32 devices in a mesh: shots: 2 (over x), blk: 16 (over z, y, core).
Axes of the slice: x: 2, y: 2, z: 4, core: 2. Of those that a mesh axis runs over, the one named last changes fastest.
Arguments:
- source_prev: float32 [32, 8, 64, 256], P(('shots', 'blk')), parts along dimension 0, may hold values from -8 to 8
- source_cur: float32 [32, 8, 64, 256], P(('shots', 'blk')), parts along dimension 0, may hold values from -8 to 8
- receiver_prev: float32 [32, 8, 64, 256], P(('shots', 'blk')), parts along dimension 0, may hold values from -8 to 8
- receiver_cur: float32 [32, 8, 64, 256], P(('shots', 'blk')), parts along dimension 0, may hold values from -8 to 8
- coef_horiz: float32 [16, 8, 64, 256], P('blk'), may hold values from 0.08 to 0.2
- coef_vert: float32 [16, 8, 64, 256], P('blk'), may hold values from 0.04 to 0.1
- coef_mixed: float32 [16, 8, 64, 256], P('blk'), may hold values from -0.05 to 0.05
- live_depth: int32 [16, 8, 64], P('blk'), may hold values from 1 to 256
- offsets: int32 [9], replicated, may hold values from 0 to 8, each once
- image_in: float32 [9, 32, 8, 64, 256], P(None, ('shots', 'blk')), parts along dimension 1, may hold values from -6 to 6
Outputs:
- image_out: float32 [9, 32, 8, 64, 256], P(None, ('shots', 'blk')), parts along dimension 1
- source_last: float32 [32, 8, 64, 256], P(('shots', 'blk')), parts along dimension 0
- receiver_last: float32 [32, 8, 64, 256], P(('shots', 'blk')), parts along dimension 0
The draws below stay inside these ranges and needn't reach their ends.
There are 2 independent parts, one for each index of `shots`. The reference program is written for one: setup_inputs(seed, part) draws one part's arguments, and reference() takes and returns one part's arrays. A program takes and returns all parts, laid end to end along the dimension named above; an argument that names none is the same for every part. Nothing has to cross between parts.
Inputs may be any that keep to these rules, and one draw needn't show every extreme that they name: offsets holds every value from 0 to 8 once.
All inputs are finite; a program needn't handle non-finite values.
Results may differ from the reference program's by a relative error of at most 0.0003.
Values sent between devices are 32-bit elements; how exact they have to be, the bound alone decides.
No kernel may reach another device: no remote copies, remote signals or barrier semaphores. Data moves between devices by JAX's collectives and lax.ppermute only.
A program may use at most 64 MiB of HBM per device.

```python
import math
import jax
import jax.numpy as jnp
from jax import lax

BX = 8
NY = 64
NZ = 256
STEPS = 4
HMAX = 4
NOFF = 9
NBLK = 16


def wave_field(key, field_salt, rough_salt):
    shape = (NBLK, BX, NY, NZ)
    envelope_key = jax.random.fold_in(key, field_salt)
    phase_key, quarter_key = jax.random.split(envelope_key, 2)
    phases = jax.random.uniform(phase_key, (2,), jnp.float32, 0.0, 2.0 * math.pi)
    quarter = jax.random.randint(quarter_key, (), 0, 4).astype(jnp.float32)
    cell_x = lax.broadcasted_iota(jnp.float32, shape, 0) * BX + lax.broadcasted_iota(jnp.float32, shape, 1)
    cell_y = lax.broadcasted_iota(jnp.float32, shape, 2)
    cell_z = lax.broadcasted_iota(jnp.float32, shape, 3)
    envelope = 1.0 + 0.15 * jnp.sin(cell_x * (2.0 * math.pi / 37.0) + phases[0]) + 0.15 * jnp.sin(cell_y * (2.0 * math.pi / 29.0) + phases[1])
    pattern = jnp.cos(cell_z * (0.5 * math.pi) + 0.25 * math.pi + 0.5 * math.pi * quarter)
    rough_key = jax.random.fold_in(key, rough_salt)
    amplitude = 5.0
    rough = 0.8 * jax.random.truncated_normal(rough_key, -3.75, 3.75, shape, jnp.float32)
    return (amplitude * envelope * pattern + rough).astype(jnp.float32)


def draw_source_prev(key, part):
    return wave_field(key, 101, 1)


def draw_source_cur(key, part):
    return wave_field(key, 101, 2)


def draw_receiver_prev(key, part):
    return wave_field(key, 202, 3)


def draw_receiver_cur(key, part):
    return wave_field(key, 202, 4)


def touch_ends(array, rng, smallest, high):
    index_at = [jax.random.randint(jax.random.fold_in(rng, axis), (), 0, length) for axis, length in enumerate(array.shape)]
    widest = array.shape.index(max(array.shape))
    beside = index_at[:widest] + [(index_at[widest] + 1) % array.shape[widest]] + index_at[widest + 1:]
    return array.at[tuple(index_at)].set(smallest).at[tuple(beside)].set(high)


def shard_levels(rng, shape, cuts, smallest, largest):
    def one(dim, shards_of):
        draws = jax.random.uniform(jax.random.fold_in(jax.random.fold_in(rng, 6), dim), (shards_of,), jnp.float32, smallest / len(cuts), largest / len(cuts))
        return jnp.repeat(jnp.exp(draws), shape[dim] // shards_of).reshape((-1,) + (1,) * (len(shape) - dim - 1))

    factor_of = one(*cuts[0])
    for cut in cuts[1:]:
        factor_of = factor_of * one(*cut)
    return factor_of


def bell_draw(key, dims, scale, reach, cuts=(), kind=jnp.bfloat16):
    level = shard_levels(key, dims, cuts, -0.22, 0.18) if cuts else 1.0
    result = jax.random.normal(key, dims, jnp.float32) * scale * level
    return jnp.minimum(jnp.maximum(result, -reach), reach).astype(kind)


def setup_inputs(seed: int = 0, part: int = 0) -> dict:
    key_of = jax.random.split(jax.random.key(seed), 11)
    part_keys = jax.random.split(jax.random.fold_in(key_of[10], part), 11)
    return {
        "source_prev": draw_source_prev(jax.random.fold_in(jax.random.fold_in(key_of[10], part), 71), part),
        "source_cur": draw_source_cur(jax.random.fold_in(jax.random.fold_in(key_of[10], part), 71), part),
        "receiver_prev": draw_receiver_prev(jax.random.fold_in(jax.random.fold_in(key_of[10], part), 71), part),
        "receiver_cur": draw_receiver_cur(jax.random.fold_in(jax.random.fold_in(key_of[10], part), 71), part),
        "coef_horiz": jnp.clip(jnp.exp(math.log(0.2) - 0.91629077 * jax.random.uniform(key_of[4], (NBLK, BX, NY, NZ), jnp.float32) ** shard_levels(key_of[4], (NBLK, BX, NY, NZ), ((0, 16),), -0.2, 0.2)), 0.08, 0.2),
        "coef_vert": jnp.clip(jnp.exp(math.log(0.1) - 0.91629077 * jax.random.uniform(key_of[5], (NBLK, BX, NY, NZ), jnp.float32) ** shard_levels(key_of[5], (NBLK, BX, NY, NZ), ((0, 16),), -0.2, 0.2)), 0.04, 0.1),
        "coef_mixed": jnp.clip(jax.random.uniform(key_of[6], (NBLK, BX, NY, NZ), jnp.float32, -0.05, 0.05) * shard_levels(key_of[6], (NBLK, BX, NY, NZ), ((0, 16),), -0.4, 0.0), -0.05, 0.05),
        "live_depth": touch_ends(jax.random.randint(key_of[7], (NBLK, BX, NY), 1, NZ + 1), jax.random.fold_in(key_of[7], 1), 1, NZ).astype(jnp.int32),
        "offsets": jax.random.permutation(key_of[8], NOFF).astype(jnp.int32),
        "image_in": bell_draw(part_keys[9], (NOFF, NBLK, BX, NY, NZ), 1.0, 6.0, ((1, 16),), jnp.float32),
    }


second_w = (-205.0 / 72.0, 8.0 / 5.0, -1.0 / 5.0, 8.0 / 315.0, -1.0 / 560.0)
first_w = (4.0 / 5.0, -1.0 / 5.0, 4.0 / 105.0, -1.0 / 280.0)


def stencil(padded_xy, coef_horiz, coef_vert, coef_mixed):
    count_x = padded_xy.shape[0] - 8
    count_y = padded_xy.shape[1] - 8
    depth = padded_xy.shape[2]
    padded = jnp.pad(padded_xy, ((0, 0), (0, 0), (4, 4)))

    def take(a, b, c):
        return padded[4 + a:4 + a + count_x, 4 + b:4 + b + count_y, 4 + c:4 + c + depth]

    center = take(0, 0, 0)
    horiz = (2.0 * second_w[0]) * center
    vert = second_w[0] * center
    deriv_z = jnp.zeros((count_x + 8, count_y, depth), jnp.float32)
    for k in range(1, 5):
        horiz = horiz + second_w[k] * (take(k, 0, 0) + take(-k, 0, 0) + take(0, k, 0) + take(0, -k, 0))
        vert = vert + second_w[k] * (take(0, 0, k) + take(0, 0, -k))
        deriv_z = deriv_z + first_w[k - 1] * (padded[:, 4:4 + count_y, 4 + k:4 + k + depth] - padded[:, 4:4 + count_y, 4 - k:4 - k + depth])
    mixed = jnp.zeros((count_x, count_y, depth), jnp.float32)
    for k in range(1, 5):
        mixed = mixed + first_w[k - 1] * (deriv_z[4 + k:4 + k + count_x] - deriv_z[4 - k:4 - k + count_x])
    return coef_horiz * horiz + coef_vert * vert + coef_mixed * mixed


def image_terms(src_pad, rec_pad, width, offsets, mute):
    count = mute.shape[0]
    terms = []
    for slot in range(NOFF):
        shift = offsets[slot] - HMAX
        left = lax.dynamic_slice_in_dim(src_pad, (width - shift).astype(jnp.int32), count, 0)
        right = lax.dynamic_slice_in_dim(rec_pad, (width + shift).astype(jnp.int32), count, 0)
        terms.append(mute * left * right)
    return jnp.stack(terms)


def to_grid(blocks):
    return blocks.reshape((NBLK * BX,) + blocks.shape[2:])


def from_grid(grid):
    return grid.reshape((NBLK, BX) + grid.shape[1:])


def step_pad(field):
    return jnp.pad(field, ((4, 4), (4, 4), (0, 0)))


def reference(source_prev, source_cur, receiver_prev, receiver_cur, coef_horiz, coef_vert, coef_mixed, live_depth, offsets, image_in):
    source_prev = to_grid(source_prev)
    source_cur = to_grid(source_cur)
    receiver_prev = to_grid(receiver_prev)
    receiver_cur = to_grid(receiver_cur)
    coef_horiz = to_grid(coef_horiz)
    coef_vert = to_grid(coef_vert)
    coef_mixed = to_grid(coef_mixed)
    depth_grid = to_grid(live_depth)
    depth_ids = lax.broadcasted_iota(jnp.int32, source_cur.shape, 2)
    mute = (depth_ids < depth_grid[:, :, None]).astype(jnp.float32)
    image = jax.vmap(to_grid)(image_in)
    for step in range(STEPS):
        src_new = 2.0 * source_cur - source_prev + stencil(step_pad(source_cur), coef_horiz, coef_vert, coef_mixed)
        rec_new = 2.0 * receiver_cur - receiver_prev + stencil(step_pad(receiver_cur), coef_horiz, coef_vert, coef_mixed)
        source_prev, source_cur = source_cur, src_new
        receiver_prev, receiver_cur = receiver_cur, rec_new
        if (step + 1) % (STEPS // 2) == 0:
            src_pad = jnp.pad(source_cur, ((HMAX, HMAX), (0, 0), (0, 0)))
            rec_pad = jnp.pad(receiver_cur, ((HMAX, HMAX), (0, 0), (0, 0)))
            image = image + image_terms(src_pad, rec_pad, HMAX, offsets, mute)
    return jax.vmap(from_grid)(image), from_grid(source_cur), from_grid(receiver_cur)
```

```python
import functools

import jax
import jax.numpy as jnp
import numpy as np
from jax import lax
from jax.experimental import pallas as pl
from jax.experimental.pallas import tpu as pltpu
from jax.sharding import PartitionSpec as P

STEPS = 4
RAD = 4
HMAX = 4
NOFF = 9

second_w = (-205.0 / 72.0, 8.0 / 5.0, -1.0 / 5.0, 8.0 / 315.0, -1.0 / 560.0)
first_w = (4.0 / 5.0, -1.0 / 5.0, 4.0 / 105.0, -1.0 / 280.0)

VMEM = pl.BlockSpec(memory_space=pltpu.VMEM)
SMEM = pl.BlockSpec(memory_space=pltpu.SMEM)
ANY = pl.BlockSpec(memory_space=pl.ANY)
MIB = 1 << 20


def parity():
    return lax.rem(lax.axis_index("blk"), 2)


def is_flipped(inner):
    odd = parity()
    return 1 - odd if inner else odd


def natural(plane, flipped):
    return plane + flipped * (7 - 2 * plane)


def at(half, other, halo, field, position):
    if position < 0:
        return halo.at[field, -1 - position]
    if position < 4:
        return half.at[field, position]
    return other.at[field, 7 - position]


def bands(depth, rows):
    d = np.arange(depth)[None, :] - np.arange(depth)[:, None]
    dzz = np.zeros((depth, depth))
    dz = np.zeros((depth, depth))
    r = np.arange(4 * rows)
    dr = np.where(r[None, :] // rows == r[:, None] // rows, r[None, :] - r[:, None], 99)
    dyy = np.zeros((4 * rows, 4 * rows))
    dzz[d == 0] = second_w[0]
    for k in range(1, 5):
        dzz[np.abs(d) == k] = second_w[k]
        dyy[np.abs(dr) == k] = second_w[k]
        dz[d == -k] = first_w[k - 1]
        dz[d == k] = -first_w[k - 1]

    def pair(m):
        m = m.astype(np.float32)
        high = m.astype(jnp.bfloat16)
        low = (m - high.astype(np.float32)).astype(jnp.bfloat16)
        return [high, low]

    return jnp.asarray(np.stack(pair(dzz) + pair(dz))), jnp.asarray(np.stack(pair(dyy)))


def gather_kernel(plan, n_in, *refs):
    ins, outs, sem = refs[:n_in], refs[n_in:-1], refs[-1]
    copies = []
    for out_id, inner, sources in plan:
        flip = is_flipped(inner)
        for i, src in enumerate(sources):
            for m in range(4):
                copies.append(
                    pltpu.make_async_copy(
                        ins[src].at[natural(m, flip)], outs[out_id].at[i, m], sem.at[len(copies)]
                    )
                )
    for c in copies:
        c.start()
    for c in copies:
        c.wait()


def gather(arrays, plan):
    shape = arrays[0].shape[1:]
    return pl.pallas_call(
        functools.partial(gather_kernel, plan, len(arrays)),
        out_shape=[jax.ShapeDtypeStruct((len(s), 4) + shape, jnp.float32) for _, _, s in plan],
        in_specs=[ANY] * len(arrays),
        out_specs=[VMEM] * len(plan),
        scratch_shapes=[pltpu.SemaphoreType.DMA((sum(4 * len(s) for _, _, s in plan),))],
        compiler_params=pltpu.CompilerParams(vmem_limit_bytes=8 * MIB),
        name="gather",
    )(*arrays)


CHUNK = 16


def step_kernel(inner, half, other, halo, prev, coef, wz, wy, out, v_hi, v_lo, x_hi, x_lo, horiz):
    rows = half.shape[2]
    sign = (1 - 2 * is_flipped(inner)).astype(jnp.float32)
    w1 = [sign * w for w in first_w]

    def first(i, carry):
        r = pl.multiple_of(i * CHUNK, CHUNK)
        span = pl.ds(r, CHUNK)
        for f in range(2):
            line = [at(half, other, halo, f, q)[span] for q in range(-4, 8)]
            for m in range(4):
                center = line[m + 4]
                hx = (2.0 * second_w[0]) * center
                dx = None
                for k in range(1, 5):
                    up, down = line[m + 4 + k], line[m + 4 - k]
                    hx = hx + second_w[k] * (up + down)
                    t = w1[k - 1] * (up - down)
                    dx = t if dx is None else dx + t
                horiz[f, m, span] = hx
                at_row = pl.ds(pl.multiple_of((f * 4 + m) * rows + r, CHUNK), CHUNK)
                high = center.astype(jnp.bfloat16)
                v_hi[at_row] = high
                v_lo[at_row] = (center - high.astype(jnp.float32)).astype(jnp.bfloat16)
                high = dx.astype(jnp.bfloat16)
                x_hi[at_row] = high
                x_lo[at_row] = (dx - high.astype(jnp.float32)).astype(jnp.bfloat16)
        return carry

    lax.fori_loop(0, rows // CHUNK, first, 0)
    dot = functools.partial(jnp.dot, preferred_element_type=jnp.float32)
    for f in range(2):
        part = pl.ds(f * 4 * rows, 4 * rows)
        vh, vl, xh, xl = v_hi[part], v_lo[part], x_hi[part], x_lo[part]
        zz = dot(vh, wz[0]) + (dot(vl, wz[0]) + dot(vh, wz[1]))
        zx = dot(xh, wz[2]) + (dot(xl, wz[2]) + dot(xh, wz[3]))
        yy = dot(wy[0], vh) + (dot(wy[0], vl) + dot(wy[1], vh))
        for m in range(4):
            cut = slice(m * rows, (m + 1) * rows)
            out[f, m] = (
                2.0 * half[f, m]
                - prev[f, m]
                + coef[0, m] * (horiz[f, m] + yy[cut])
                + coef[1, m] * zz[cut]
                + coef[2, m] * zx[cut]
            )


def step(inner, half, other, halo, prev, coef, wz, wy):
    rows, depth = half.shape[2:]
    flat = pltpu.VMEM((8 * rows, depth), jnp.bfloat16)
    return pl.pallas_call(
        functools.partial(step_kernel, inner),
        out_shape=jax.ShapeDtypeStruct(half.shape, jnp.float32),
        in_specs=[VMEM] * 7,
        out_specs=VMEM,
        scratch_shapes=[flat] * 4 + [pltpu.VMEM(half.shape, jnp.float32)],
        compiler_params=pltpu.CompilerParams(vmem_limit_bytes=12 * MIB),
        name="inner_step" if inner else "outer_step",
    )(half, other, halo, prev, coef, wz, wy)


def find_slots(offsets, slots):
    for k in range(NOFF):
        slots[offsets[k]] = k


def add_terms(acc, slots, mute, snaps, inner, wanted):
    flip = is_flipped(inner)
    sign = 1 - 2 * flip
    slot = {h: slots[sign * h + HMAX] for h in range(-HMAX, HMAX + 1)}
    places = [natural(m, flip) for m in range(4)]
    locals_ = [m + flip * (3 - 2 * m) for m in range(4)]
    rows = acc.shape[2]

    def body(i, carry):
        span = pl.ds(pl.multiple_of(i * 8, 8), 8)
        for m in range(4):
            mask = mute[places[m], span]
            for h in range(-HMAX, HMAX + 1):
                if not wanted(h, m):
                    continue
                total = None
                for half, other, halo in snaps:
                    t = at(half, other, halo, 0, m - h)[span] * at(half, other, halo, 1, m + h)[span]
                    total = t if total is None else total + t
                acc[slot[h], locals_[m], span] += mask * total
        return carry

    lax.fori_loop(0, rows // 8, body, 0)


def half_planes(image, inner):
    return image.at[:, pl.ds(4 * is_flipped(inner), 4)]


def image_mid_kernel(image_in, offsets, mute, half, other, halo, acc, slots, sem):
    copy = pltpu.make_async_copy(half_planes(image_in, False), acc, sem)
    copy.start()
    find_slots(offsets, slots)
    copy.wait()
    add_terms(acc, slots, mute, [(half, other, halo)], False, lambda h, m: True)


def image_mid(image_in, offsets, mute, half, other, halo):
    shape = (NOFF, 4) + half.shape[2:]
    return pl.pallas_call(
        image_mid_kernel,
        out_shape=jax.ShapeDtypeStruct(shape, jnp.float32),
        in_specs=[ANY, SMEM] + [VMEM] * 4,
        out_specs=VMEM,
        scratch_shapes=[pltpu.SMEM((NOFF,), jnp.int32), pltpu.SemaphoreType.DMA],
        compiler_params=pltpu.CompilerParams(vmem_limit_bytes=8 * MIB),
        name="image_mid",
    )(image_in, offsets, mute, half, other, halo)


def image_inner_kernel(
    image_in, offsets, mute, in2, out2, hal2, in4, out4, hal4, image, src, rec, acc, slots, sem, sems
):
    fetch = pltpu.make_async_copy(half_planes(image_in, True), acc, sem)
    fetch.start()
    copies = []
    for inner, field4 in ((True, in4), (False, out4)):
        for f, last in ((0, src), (1, rec)):
            for m in range(4):
                copies.append(
                    pltpu.make_async_copy(
                        field4.at[f, m], last.at[natural(m, is_flipped(inner))], sems.at[len(copies)]
                    )
                )
    for c in copies:
        c.start()
    find_slots(offsets, slots)
    fetch.wait()
    add_terms(
        acc, slots, mute, [(in2, out2, hal2), (in4, out4, hal4)], True, lambda h, m: True
    )
    store = pltpu.make_async_copy(acc, half_planes(image, True), sem)
    store.start()
    for c in copies:
        c.wait()
    store.wait()


def image_inner(image_in, offsets, mute, snap2, snap4):
    shape = snap2[0].shape
    field = jax.ShapeDtypeStruct((8,) + shape[2:], jnp.float32)
    return pl.pallas_call(
        image_inner_kernel,
        out_shape=[jax.ShapeDtypeStruct(image_in.shape, jnp.float32), field, field],
        in_specs=[ANY, SMEM] + [VMEM] * 7,
        out_specs=[ANY] * 3,
        scratch_shapes=[
            pltpu.VMEM((NOFF, 4) + shape[2:], jnp.float32),
            pltpu.SMEM((NOFF,), jnp.int32),
            pltpu.SemaphoreType.DMA,
            pltpu.SemaphoreType.DMA((16,)),
        ],
        compiler_params=pltpu.CompilerParams(vmem_limit_bytes=8 * MIB),
        name="image_inner",
    )(image_in, offsets, mute, *snap2, *snap4)


def image_last_kernel(image_old, part, offsets, mute, half, other, halo, image, acc, slots, sem):
    del image_old
    find_slots(offsets, slots)
    acc[...] = part[...]
    add_terms(acc, slots, mute, [(half, other, halo)], False, lambda h, m: True)
    store = pltpu.make_async_copy(acc, half_planes(image, False), sem)
    store.start()
    store.wait()


def image_last(image, part, offsets, mute, snap4):
    return pl.pallas_call(
        image_last_kernel,
        out_shape=jax.ShapeDtypeStruct(image.shape, jnp.float32),
        in_specs=[ANY, VMEM, SMEM] + [VMEM] * 4,
        out_specs=ANY,
        scratch_shapes=[
            pltpu.VMEM(part.shape, jnp.float32),
            pltpu.SMEM((NOFF,), jnp.int32),
            pltpu.SemaphoreType.DMA,
        ],
        input_output_aliases={0: 0},
        compiler_params=pltpu.CompilerParams(vmem_limit_bytes=8 * MIB),
        name="image_last",
    )(image, part, offsets, mute, *snap4)


def across_chips(value):
    count = lax.axis_size("blk")
    pairs = [(i, i + 1) for i in range(1, count - 1, 2)]
    return lax.ppermute(value, "blk", pairs + [(b, a) for a, b in pairs])


def within_chip(value):
    return lax.ppermute(value, "blk", [(i, i ^ 1) for i in range(lax.axis_size("blk"))])


def per_device(
    source_prev,
    source_cur,
    receiver_prev,
    receiver_cur,
    coef_horiz,
    coef_vert,
    coef_mixed,
    live_depth,
    offsets,
    image_in,
):
    source_prev, source_cur = source_prev[0], source_cur[0]
    receiver_prev, receiver_cur = receiver_prev[0], receiver_cur[0]
    coefs = [coef_horiz[0], coef_vert[0], coef_mixed[0]]
    image_in = image_in[:, 0]
    rows, depth = source_cur.shape[1:]
    wz, wy = bands(depth, rows)
    depth_ids = lax.broadcasted_iota(jnp.int32, source_cur.shape, 2)
    mute = (depth_ids < live_depth[0][:, :, None]).astype(jnp.float32)

    (out,) = gather([source_cur, receiver_cur], [(0, False, (0, 1))])
    far = across_chips(out)
    inn, prev_out, prev_inn, coef_out, coef_inn = gather(
        [source_cur, receiver_cur, source_prev, receiver_prev] + coefs,
        [
            (0, True, (0, 1)),
            (1, False, (2, 3)),
            (2, True, (2, 3)),
            (3, False, (4, 5, 6)),
            (4, True, (4, 5, 6)),
        ],
    )
    near = within_chip(inn)
    acc = None
    for n in range(STEPS):
        new_inn = step(True, inn, out, near, prev_inn, coef_inn, wz, wy)
        new_out = step(False, out, inn, far, prev_out, coef_out, wz, wy)
        if n == STEPS // 2:
            snap2 = (inn, out, near)
            part = image_mid(image_in, offsets, mute, out, inn, far)
        prev_inn, prev_out, inn, out = inn, out, new_inn, new_out
        near = within_chip(inn)
        far = across_chips(out)
    image, source_last, receiver_last = image_inner(
        image_in, offsets, mute, snap2, (inn, out, near)
    )
    image = image_last(image, part, offsets, mute, (out, inn, far))
    return (image[:, None], source_last[None], receiver_last[None])


def solution(mesh):
    in_specs = (
        P(("shots", "blk"), None, None, None),
        P(("shots", "blk"), None, None, None),
        P(("shots", "blk"), None, None, None),
        P(("shots", "blk"), None, None, None),
        P("blk", None, None, None),
        P("blk", None, None, None),
        P("blk", None, None, None),
        P("blk", None, None),
        P(),
        P(None, ("shots", "blk"), None, None, None),
    )
    out_specs = (
        P(None, ("shots", "blk"), None, None, None),
        P(("shots", "blk"), None, None, None),
        P(("shots", "blk"), None, None, None),
    )
    return jax.shard_map(
        per_device, mesh=mesh, in_specs=in_specs, out_specs=out_specs, check_vma=False
    )
```

```python
import functools

import jax
import jax.numpy as jnp
import numpy as np
from jax import lax
from jax.experimental import pallas as pl
from jax.experimental.pallas import tpu as pltpu
from jax.sharding import PartitionSpec as P

STEPS = 4
RAD = 4
HMAX = 4
NOFF = 9

second_w = (-205.0 / 72.0, 8.0 / 5.0, -1.0 / 5.0, 8.0 / 315.0, -1.0 / 560.0)
first_w = (4.0 / 5.0, -1.0 / 5.0, 4.0 / 105.0, -1.0 / 280.0)

VMEM = pl.BlockSpec(memory_space=pltpu.VMEM)
SMEM = pl.BlockSpec(memory_space=pltpu.SMEM)
ANY = pl.BlockSpec(memory_space=pl.ANY)
HBM = pl.BlockSpec(memory_space=pltpu.HBM)
MIB = 1 << 20
CHEAP = pl.CostEstimate(flops=1, transcendentals=0, bytes_accessed=1)


def parity():
    return lax.rem(lax.axis_index("blk"), 2)


def is_flipped(inner):
    odd = parity()
    return 1 - odd if inner else odd


def natural(plane, flipped):
    return plane + flipped * (7 - 2 * plane)


def at(half, other, halo, field, position):
    if position < 0:
        return halo.at[field, -1 - position]
    if position < 4:
        return half.at[field, position]
    return other.at[field, 7 - position]


SCALE = 5040
second_int = tuple(round(SCALE * w) for w in second_w)
first_int = tuple(round(840 * w) for w in first_w)
mixed_w = tuple(SCALE / 840 * w for w in first_w)


def bands(depth, rows):
    d = np.arange(depth)[None, :] - np.arange(depth)[:, None]
    r = np.arange(4 * rows)
    dr = np.where(r[None, :] // rows == r[:, None] // rows, r[None, :] - r[:, None], 99)
    dzz, dz = np.zeros(d.shape), np.zeros(d.shape)
    dyy = np.zeros(dr.shape)
    for k in range(1, 5):
        dzz[np.abs(d) == k] = second_int[k]
        dyy[np.abs(dr) == k] = second_int[k]
        dz[d == -k] = first_int[k - 1]
        dz[d == k] = -first_int[k - 1]
    return jnp.asarray(np.stack([dzz, dz]).astype(jnp.bfloat16)), jnp.asarray(dyy.astype(jnp.bfloat16))


def gather_kernel(plan, n_in, *refs):
    ins, outs, sem = refs[:n_in], refs[n_in:-1], refs[-1]
    copies = []
    for out_id, inner, sources in plan:
        flip = is_flipped(inner)
        for i, src in enumerate(sources):
            for m in range(4):
                copies.append(
                    pltpu.make_async_copy(
                        ins[src].at[natural(m, flip)], outs[out_id].at[i, m], sem.at[len(copies)]
                    )
                )
    for c in copies:
        c.start()
    for c in copies:
        c.wait()


def gather(arrays, plan):
    shape = arrays[0].shape[1:]
    arrays = [pltpu.with_memory_space_constraint(a, pltpu.HBM) for a in arrays]
    return pl.pallas_call(
        functools.partial(gather_kernel, plan, len(arrays)),
        out_shape=[jax.ShapeDtypeStruct((len(s), 4) + shape, jnp.float32) for _, _, s in plan],
        in_specs=[HBM] * len(arrays),
        out_specs=[VMEM] * len(plan),
        scratch_shapes=[pltpu.SemaphoreType.DMA((sum(4 * len(s) for _, _, s in plan),))],
        cost_estimate=CHEAP,
        compiler_params=pltpu.CompilerParams(vmem_limit_bytes=8 * MIB),
        name="gather",
    )(*arrays)


CHUNK = 16
dot = functools.partial(jnp.dot, preferred_element_type=jnp.float32)


def split(value):
    high = value.astype(jnp.bfloat16)
    return high, (value - high.astype(jnp.float32)).astype(jnp.bfloat16)


def advance(inner, half, other, halo, prev, coef, wz, wy, out, v_hi, v_lo, x_hi, x_lo, horiz):
    rows = half.shape[2]
    sign = (1 - 2 * is_flipped(inner)).astype(jnp.float32)
    wx = [sign * w for w in mixed_w]

    def first(i, carry):
        r = pl.multiple_of(i * CHUNK, CHUNK)
        span = pl.ds(r, CHUNK)
        for f in range(2):
            low = 0 if halo is None else -4
            line = {q: at(half, other, halo, f, q)[span] for q in range(low, 8)}
            for m in range(4):
                center = line[m]
                hx = (2.0 * SCALE * second_w[0]) * center
                dx = None
                for k in range(1, 5):
                    up = line[m + k]
                    if m - k in line:
                        both, t = up + line[m - k], up - line[m - k]
                    else:
                        both, t = up, up
                    hx = hx + float(second_int[k]) * both
                    t = wx[k - 1] * t
                    dx = t if dx is None else dx + t
                horiz[f, m, span] = hx
                at_row = pl.ds(pl.multiple_of((f * 4 + m) * rows + r, CHUNK), CHUNK)
                v_hi[at_row], v_lo[at_row] = split(center)
                x_hi[at_row], x_lo[at_row] = split(dx)
        return carry

    lax.fori_loop(0, rows // CHUNK, first, 0)
    for f in range(2):
        part = pl.ds(f * 4 * rows, 4 * rows)
        vh, vl, xh, xl = v_hi[part], v_lo[part], x_hi[part], x_lo[part]
        zz = dot(vh, wz[0]) + dot(vl, wz[0])
        zx = dot(xh, wz[1]) + dot(xl, wz[1])
        yy = dot(wy[...], vh) + dot(wy[...], vl)
        for m in range(4):
            cut = slice(m * rows, (m + 1) * rows)
            center = half[f, m]
            out[f, m] = (
                2.0 * center
                - prev[f, m]
                + (1.0 / SCALE)
                * (
                    coef[0, m] * (horiz[f, m] + yy[cut])
                    + coef[1, m] * (zz[cut] + (SCALE * second_w[0]) * center)
                    + coef[2, m] * zx[cut]
                )
            )


def under_kernel(
    inn, out, near, prev_inn, prev_out, coef_inn, coef_out, wz, wy, new_inn, base, *scratch
):
    advance(True, inn, out, near, prev_inn, coef_inn, wz, wy, new_inn, *scratch)
    advance(False, out, inn, None, prev_out, coef_out, wz, wy, base, *scratch)


def first_under_kernel(
    inn, out, near, wz, wy, source_prev, receiver_prev, coef_a, coef_b, coef_c,
    new_inn, base, coef_inn, coef_out, prev_inn, prev_out, sem, *scratch
):
    prevs = (source_prev, receiver_prev)
    coefs = (coef_a, coef_b, coef_c)
    copies = []
    for inner, prev, coef in ((True, prev_inn, coef_inn), (False, prev_out, coef_out)):
        for sources, target in ((coefs, coef), (prevs, prev)):
            for i, source in enumerate(sources):
                for m in range(4):
                    copies.append(
                        pltpu.make_async_copy(
                            source.at[natural(m, is_flipped(inner))], target.at[i, m], sem.at[len(copies)]
                        )
                    )
    for c in copies:
        c.start()
    for c in copies[:20]:
        c.wait()
    advance(True, inn, out, near, prev_inn, coef_inn, wz, wy, new_inn, *scratch)
    for c in copies[20:]:
        c.wait()
    advance(False, out, inn, None, prev_out, coef_out, wz, wy, base, *scratch)


def work_space(rows, depth):
    flat = pltpu.VMEM((8 * rows, depth), jnp.bfloat16)
    return [flat] * 4 + [pltpu.VMEM((2, 4, rows, depth), jnp.float32)]


def first_under(inn, out, near, wz, wy, arrays):
    rows, depth = inn.shape[2:]
    arrays = [pltpu.with_memory_space_constraint(a, pltpu.HBM) for a in arrays]
    pair = jax.ShapeDtypeStruct((2, 4, rows, depth), jnp.float32)
    three = jax.ShapeDtypeStruct((3, 4, rows, depth), jnp.float32)
    half = pltpu.VMEM((2, 4, rows, depth), jnp.float32)
    return pl.pallas_call(
        first_under_kernel,
        out_shape=[pair, pair, three, three],
        in_specs=[VMEM] * 5 + [HBM] * 5,
        out_specs=[VMEM] * 4,
        scratch_shapes=[half, half, pltpu.SemaphoreType.DMA((40,))] + work_space(rows, depth),
        cost_estimate=CHEAP,
        compiler_params=pltpu.CompilerParams(vmem_limit_bytes=12 * MIB),
        name="first_under",
    )(inn, out, near, wz, wy, *arrays)


def under(inn, out, near, prev_inn, prev_out, coef_inn, coef_out, wz, wy):
    shape = jax.ShapeDtypeStruct(inn.shape, jnp.float32)
    return pl.pallas_call(
        under_kernel,
        out_shape=[shape, shape],
        in_specs=[VMEM] * 9,
        out_specs=[VMEM] * 2,
        scratch_shapes=work_space(*inn.shape[2:]),
        cost_estimate=CHEAP,
        compiler_params=pltpu.CompilerParams(vmem_limit_bytes=12 * MIB),
        name="under",
    )(inn, out, near, prev_inn, prev_out, coef_inn, coef_out, wz, wy)


def finish_kernel(halo, base, coef, wz, out, hi, lo):
    rows = halo.shape[2]
    sign = (1 - 2 * is_flipped(False)).astype(jnp.float32)
    wx = [sign * w for w in mixed_w]
    for f in range(2):
        for j in range(4):
            at_row = pl.ds((f * 4 + j) * rows, rows)
            hi[at_row], lo[at_row] = split(halo[f, j])
    for f in range(2):
        part = pl.ds(f * 4 * rows, 4 * rows)
        dz = dot(hi[part], wz[1]) + dot(lo[part], wz[1])
        for m in range(4):
            hx = zx = None
            for k in range(m + 1, 5):
                j = k - m - 1
                t = float(second_int[k]) * halo[f, j]
                hx = t if hx is None else hx + t
                t = wx[k - 1] * dz[j * rows : (j + 1) * rows]
                zx = t if zx is None else zx + t
            out[f, m] = base[f, m] + (1.0 / SCALE) * (coef[0, m] * hx - coef[2, m] * zx)


def finish(halo, base, coef, wz):
    rows, depth = halo.shape[2:]
    return pl.pallas_call(
        finish_kernel,
        out_shape=jax.ShapeDtypeStruct(halo.shape, jnp.float32),
        in_specs=[VMEM] * 4,
        out_specs=VMEM,
        scratch_shapes=[pltpu.VMEM((8 * rows, depth), jnp.bfloat16)] * 2,
        cost_estimate=CHEAP,
        compiler_params=pltpu.CompilerParams(vmem_limit_bytes=8 * MIB),
        name="finish",
    )(halo, base, coef, wz)


def find_slots(offsets, slots):
    for k in range(NOFF):
        slots[offsets[k]] = k


def slot_of(slots, inner, h):
    return slots[(1 - 2 * is_flipped(inner)) * h + HMAX]


BY_REACH = (-4, 4, -3, 3, -2, 2, -1, 1, 0)


def add_terms(old, new, slot, h, planes, mute, snaps, inner):
    flip = is_flipped(inner)
    rows = old.shape[2]

    def body(i, carry):
        span = pl.ds(pl.multiple_of(i * CHUNK, CHUNK), CHUNK)
        for m in planes:
            total = None
            for half, other, halo in snaps:
                t = at(half, other, halo, 0, m - h)[span] * at(half, other, halo, 1, m + h)[span]
                total = t if total is None else total + t
            local = m + flip * (3 - 2 * m)
            new[slot, local, span] = old[slot, local, span] + mute[natural(m, flip), span] * total
        return carry

    lax.fori_loop(0, rows // CHUNK, body, 0)


def store_planes(buffer, image, slot, first, count, inner, sem):
    flip = is_flipped(inner)
    start = first + flip * (4 - 2 * first - count)
    return pltpu.make_async_copy(
        buffer.at[slot, pl.ds(start, count)], image.at[slot, pl.ds(4 * flip + start, count)], sem
    )


def image_mid_kernel(image_in, offsets, mute, half, other, halo, acc, slots, sem):
    find_slots(offsets, slots)
    near = pl.ds(4 * is_flipped(False), 4)
    slot = [slot_of(slots, False, h) for h in BY_REACH]
    copies = [
        pltpu.make_async_copy(image_in.at[k, near], acc.at[k], sem.at[i])
        for i, k in enumerate(slot)
    ]
    for c in copies:
        c.start()
    for i, h in enumerate(BY_REACH):
        copies[i].wait()
        add_terms(acc, acc, slot[i], h, range(4), mute, [(half, other, halo)], False)


def image_mid(image_in, offsets, mute, half, other, halo):
    shape = (NOFF, 4) + half.shape[2:]
    return pl.pallas_call(
        image_mid_kernel,
        out_shape=jax.ShapeDtypeStruct(shape, jnp.float32),
        in_specs=[HBM, SMEM] + [VMEM] * 4,
        out_specs=VMEM,
        scratch_shapes=[pltpu.SMEM((NOFF,), jnp.int32), pltpu.SemaphoreType.DMA((NOFF,))],
        cost_estimate=CHEAP,
        compiler_params=pltpu.CompilerParams(vmem_limit_bytes=8 * MIB),
        name="image_mid",
    )(image_in, offsets, mute, half, other, halo)


def image_main_kernel(
    image_in, part, offsets, mute, in2, out2, hal2, in4, out4, hal4,
    image, src, rec, acc, done, slots, sem, sems,
):
    find_slots(offsets, slots)
    inner_half = pl.ds(4 * is_flipped(True), 4)
    inner_slot = [slot_of(slots, True, h) for h in BY_REACH]
    outer_slot = [slot_of(slots, False, h) for h in BY_REACH]
    fetches = [
        pltpu.make_async_copy(image_in.at[k, inner_half], acc.at[k], sem.at[i])
        for i, k in enumerate(inner_slot)
    ]
    for c in fetches:
        c.start()
    copies = []
    for inner, field4 in ((True, in4), (False, out4)):
        for f, last in ((0, src), (1, rec)):
            for m in range(4):
                copies.append(
                    pltpu.make_async_copy(
                        field4.at[f, m], last.at[natural(m, is_flipped(inner))], sems.at[len(copies)]
                    )
                )
    for c in copies:
        c.start()
    stores = []
    for i, h in enumerate(BY_REACH):
        reach = abs(h)
        if reach == 4:
            continue
        k = outer_slot[i]
        add_terms(part, done, k, h, range(reach, 4), mute, [(out4, in4, None)], False)
        stores.append(store_planes(done, image, k, reach, 4 - reach, False, sem.at[NOFF + i]))
        stores[-1].start()
    for i, h in enumerate(BY_REACH):
        fetches[i].wait()
        k = inner_slot[i]
        add_terms(acc, acc, k, h, range(4), mute, [(in2, out2, hal2), (in4, out4, hal4)], True)
        stores.append(store_planes(acc, image, k, 0, 4, True, sem.at[i]))
        stores[-1].start()
    for c in copies + stores:
        c.wait()


def image_main(image_in, part, offsets, mute, snap2, snap4):
    shape = snap2[0].shape
    field = jax.ShapeDtypeStruct((8,) + shape[2:], jnp.float32)
    return pl.pallas_call(
        image_main_kernel,
        out_shape=[jax.ShapeDtypeStruct(image_in.shape, jnp.float32), field, field],
        in_specs=[HBM, VMEM, SMEM] + [VMEM] * 7,
        out_specs=[HBM] * 3,
        scratch_shapes=[
            pltpu.VMEM(part.shape, jnp.float32),
            pltpu.VMEM(part.shape, jnp.float32),
            pltpu.SMEM((NOFF,), jnp.int32),
            pltpu.SemaphoreType.DMA((2 * NOFF,)),
            pltpu.SemaphoreType.DMA((16,)),
        ],
        cost_estimate=CHEAP,
        compiler_params=pltpu.CompilerParams(vmem_limit_bytes=8 * MIB),
        name="image_main",
    )(image_in, part, offsets, mute, *snap2, *snap4)


def image_last_kernel(image_old, part, offsets, mute, half, other, halo, image, done, slots, sem):
    del image_old
    find_slots(offsets, slots)
    stores = []
    for i, h in enumerate(BY_REACH[:-1]):
        reach = abs(h)
        k = slot_of(slots, False, h)
        add_terms(part, done, k, h, range(reach), mute, [(half, other, halo)], False)
        stores.append(store_planes(done, image, k, 0, reach, False, sem.at[i]))
        stores[-1].start()
    for c in stores:
        c.wait()


def image_last(image, part, offsets, mute, snap4):
    return pl.pallas_call(
        image_last_kernel,
        out_shape=jax.ShapeDtypeStruct(image.shape, jnp.float32),
        in_specs=[HBM, VMEM, SMEM] + [VMEM] * 4,
        out_specs=HBM,
        scratch_shapes=[
            pltpu.VMEM(part.shape, jnp.float32),
            pltpu.SMEM((NOFF,), jnp.int32),
            pltpu.SemaphoreType.DMA((NOFF,)),
        ],
        input_output_aliases={0: 0},
        cost_estimate=CHEAP,
        compiler_params=pltpu.CompilerParams(vmem_limit_bytes=8 * MIB),
        name="image_last",
    )(image, part, offsets, mute, *snap4)


def across_chips(value, start=1, stride=2):
    count = lax.axis_size("blk")
    pairs = [(i, i + 1) for i in range(start, count - 1, stride)]
    return lax.ppermute(value, "blk", pairs + [(b, a) for a, b in pairs])


def within_chip(value):
    return lax.ppermute(value, "blk", [(i, i ^ 1) for i in range(lax.axis_size("blk"))])


def per_device(
    source_prev,
    source_cur,
    receiver_prev,
    receiver_cur,
    coef_horiz,
    coef_vert,
    coef_mixed,
    live_depth,
    offsets,
    image_in,
):
    source_prev, source_cur = source_prev[0], source_cur[0]
    receiver_prev, receiver_cur = receiver_prev[0], receiver_cur[0]
    coefs = [coef_horiz[0], coef_vert[0], coef_mixed[0]]
    image_in = image_in[:, 0]
    rows, depth = source_cur.shape[1:]
    wz, wy = bands(depth, rows)
    depth_ids = lax.broadcasted_iota(jnp.int32, source_cur.shape, 2)
    mute = (depth_ids < live_depth[0][:, :, None]).astype(jnp.float32)

    out, inn = gather([source_cur, receiver_cur], [(0, False, (0, 1)), (1, True, (0, 1))])
    far = across_chips(out)
    near = within_chip(inn)
    new_inn, base, coef_inn, coef_out = first_under(
        inn, out, near, wz, wy, [source_prev, receiver_prev] + coefs
    )
    for n in range(STEPS):
        if n == STEPS // 2 + 1:
            inn, part = lax.optimization_barrier((inn, part))
        if n > 0:
            new_inn, base = under(inn, out, near, prev_inn, prev_out, coef_inn, coef_out, wz, wy)
        new_out = finish(far, base, coef_out, wz)
        if n == STEPS // 2:
            snap2 = (inn, out, near)
            part = image_mid(image_in, offsets, mute, out, inn, far)
        prev_inn, prev_out, inn, out = inn, out, new_inn, new_out
        near = within_chip(inn)
        far = across_chips(out)
    image, source_last, receiver_last = image_main(
        image_in, part, offsets, mute, snap2, (inn, out, near)
    )
    image = image_last(image, part, offsets, mute, (out, inn, far))
    return (image[:, None], source_last[None], receiver_last[None])


def solution(mesh):
    in_specs = (
        P(("shots", "blk"), None, None, None),
        P(("shots", "blk"), None, None, None),
        P(("shots", "blk"), None, None, None),
        P(("shots", "blk"), None, None, None),
        P("blk", None, None, None),
        P("blk", None, None, None),
        P("blk", None, None, None),
        P("blk", None, None),
        P(),
        P(None, ("shots", "blk"), None, None, None),
    )
    out_specs = (
        P(None, ("shots", "blk"), None, None, None),
        P(("shots", "blk"), None, None, None),
        P(("shots", "blk"), None, None, None),
    )
    return jax.shard_map(
        per_device, mesh=mesh, in_specs=in_specs, out_specs=out_specs, check_vma=False
    )
```

```python
import functools

import jax
import jax.numpy as jnp
import numpy as np
from jax import lax
from jax.experimental import pallas as pl
from jax.experimental.pallas import tpu as pltpu
from jax.sharding import PartitionSpec as P

STEPS = 4
RAD = 4
HMAX = 4
NOFF = 9

second_w = (-205.0 / 72.0, 8.0 / 5.0, -1.0 / 5.0, 8.0 / 315.0, -1.0 / 560.0)
first_w = (4.0 / 5.0, -1.0 / 5.0, 4.0 / 105.0, -1.0 / 280.0)

VMEM = pl.BlockSpec(memory_space=pltpu.VMEM)
SMEM = pl.BlockSpec(memory_space=pltpu.SMEM)
ANY = pl.BlockSpec(memory_space=pl.ANY)
HBM = pl.BlockSpec(memory_space=pltpu.HBM)
MIB = 1 << 20
CHEAP = pl.CostEstimate(flops=1, transcendentals=0, bytes_accessed=1)


def parity():
    return lax.rem(lax.axis_index("blk"), 2)


def is_flipped(inner):
    odd = parity()
    return 1 - odd if inner else odd


def natural(plane, flipped):
    return plane + flipped * (7 - 2 * plane)


def at(half, other, halo, field, position):
    if position < 0:
        return halo.at[field, -1 - position]
    if position < 4:
        return half.at[field, position]
    return other.at[field, 7 - position]


SCALE = 5040
second_int = tuple(round(SCALE * w) for w in second_w)
first_int = tuple(round(840 * w) for w in first_w)
mixed_w = tuple(SCALE / 840 * w for w in first_w)


def bands(depth, rows):
    d = np.arange(depth)[None, :] - np.arange(depth)[:, None]
    r = np.arange(4 * rows)
    dr = np.where(r[None, :] // rows == r[:, None] // rows, r[None, :] - r[:, None], 99)
    dzz, dz = np.zeros(d.shape), np.zeros(d.shape)
    dyy = np.zeros(dr.shape)
    for k in range(1, 5):
        dzz[np.abs(d) == k] = second_int[k]
        dyy[np.abs(dr) == k] = second_int[k]
        dz[d == -k] = first_int[k - 1]
        dz[d == k] = -first_int[k - 1]
    return jnp.asarray(np.stack([dzz, dz]).astype(jnp.bfloat16)), jnp.asarray(dyy.astype(jnp.bfloat16))


def gather_kernel(plan, n_in, *refs):
    ins, outs, sem = refs[:n_in], refs[n_in:-1], refs[-1]
    copies = []
    for out_id, inner, sources in plan:
        flip = is_flipped(inner)
        for i, src in enumerate(sources):
            for m in range(4):
                copies.append(
                    pltpu.make_async_copy(
                        ins[src].at[natural(m, flip)], outs[out_id].at[i, m], sem.at[len(copies)]
                    )
                )
    for c in copies:
        c.start()
    for c in copies:
        c.wait()


def gather(arrays, plan):
    shape = arrays[0].shape[1:]
    arrays = [pltpu.with_memory_space_constraint(a, pltpu.HBM) for a in arrays]
    return pl.pallas_call(
        functools.partial(gather_kernel, plan, len(arrays)),
        out_shape=[jax.ShapeDtypeStruct((len(s), 4) + shape, jnp.float32) for _, _, s in plan],
        in_specs=[HBM] * len(arrays),
        out_specs=[VMEM] * len(plan),
        scratch_shapes=[pltpu.SemaphoreType.DMA((sum(4 * len(s) for _, _, s in plan),))],
        cost_estimate=CHEAP,
        compiler_params=pltpu.CompilerParams(vmem_limit_bytes=8 * MIB),
        name="gather",
    )(*arrays)


CHUNK = 16
dot = functools.partial(jnp.dot, preferred_element_type=jnp.float32)


def split(value):
    high = value.astype(jnp.bfloat16)
    return high, (value - high.astype(jnp.float32)).astype(jnp.bfloat16)


def advance(inner, half, other, halo, prev, coef, wz, wy, out, v_hi, v_lo, x_hi, x_lo, horiz):
    rows = half.shape[2]
    sign = (1 - 2 * is_flipped(inner)).astype(jnp.float32)
    wx = [sign * w for w in mixed_w]

    for f in range(2):
        for r in range(0, rows, CHUNK):
            span = pl.ds(r, CHUNK)
            low = 0 if halo is None else -4
            line = {q: at(half, other, halo, f, q)[span] for q in range(low, 8)}
            for m in range(4):
                center = line[m]
                hx = (2.0 * SCALE * second_w[0]) * center
                dx = None
                for k in range(1, 5):
                    up = line[m + k]
                    if m - k in line:
                        both, t = up + line[m - k], up - line[m - k]
                    else:
                        both, t = up, up
                    hx = hx + float(second_int[k]) * both
                    t = wx[k - 1] * t
                    dx = t if dx is None else dx + t
                horiz[f, m, span] = hx
                at_row = pl.ds((f * 4 + m) * rows + r, CHUNK)
                v_hi[at_row], v_lo[at_row] = split(center)
                x_hi[at_row], x_lo[at_row] = split(dx)
        part = pl.ds(f * 4 * rows, 4 * rows)
        vh, vl, xh, xl = v_hi[part], v_lo[part], x_hi[part], x_lo[part]
        zz = dot(vh, wz[0]) + dot(vl, wz[0])
        zx = dot(xh, wz[1]) + dot(xl, wz[1])
        yy = dot(wy[...], vh) + dot(wy[...], vl)
        for m in range(4):
            cut = slice(m * rows, (m + 1) * rows)
            center = half[f, m]
            out[f, m] = (
                2.0 * center
                - prev[f, m]
                + (1.0 / SCALE)
                * (
                    coef[0, m] * (horiz[f, m] + yy[cut])
                    + coef[1, m] * (zz[cut] + (SCALE * second_w[0]) * center)
                    + coef[2, m] * zx[cut]
                )
            )


def inner_kernel(inn, out, near, prev_inn, coef_inn, wz, wy, new_inn, *scratch):
    advance(True, inn, out, near, prev_inn, coef_inn, wz, wy, new_inn, *scratch)


def base_kernel(out, inn, prev_out, coef_out, wz, wy, base, *scratch):
    advance(False, out, inn, None, prev_out, coef_out, wz, wy, base, *scratch)


def first_kernel(
    inn, out, near, wz, wy, source_prev, receiver_prev, coef_a, coef_b, coef_c,
    new_inn, base, coef_inn, coef_out, prev_inn, prev_out, sem, *scratch
):
    prevs = (source_prev, receiver_prev)
    coefs = (coef_a, coef_b, coef_c)
    copies = []
    for inner, prev, coef in ((True, prev_inn, coef_inn), (False, prev_out, coef_out)):
        for sources, target in ((coefs, coef), (prevs, prev)):
            for i, source in enumerate(sources):
                for m in range(4):
                    copies.append(
                        pltpu.make_async_copy(
                            source.at[natural(m, is_flipped(inner))], target.at[i, m], sem.at[len(copies)]
                        )
                    )
    for c in copies:
        c.start()
    for c in copies[:20]:
        c.wait()
    advance(True, inn, out, near, prev_inn, coef_inn, wz, wy, new_inn, *scratch)
    for c in copies[20:]:
        c.wait()
    advance(False, out, inn, None, prev_out, coef_out, wz, wy, base, *scratch)


def work_space(rows, depth):
    flat = pltpu.VMEM((8 * rows, depth), jnp.bfloat16)
    return [flat] * 4 + [pltpu.VMEM((2, 4, rows, depth), jnp.float32)]


def first(inn, out, near, wz, wy, arrays):
    rows, depth = inn.shape[2:]
    arrays = [pltpu.with_memory_space_constraint(a, pltpu.HBM) for a in arrays]
    pair = jax.ShapeDtypeStruct((2, 4, rows, depth), jnp.float32)
    three = jax.ShapeDtypeStruct((3, 4, rows, depth), jnp.float32)
    half = pltpu.VMEM((2, 4, rows, depth), jnp.float32)
    return pl.pallas_call(
        first_kernel,
        out_shape=[pair, pair, three, three],
        in_specs=[VMEM] * 5 + [HBM] * 5,
        out_specs=[VMEM] * 4,
        scratch_shapes=[half, half, pltpu.SemaphoreType.DMA((40,))] + work_space(rows, depth),
        cost_estimate=CHEAP,
        compiler_params=pltpu.CompilerParams(vmem_limit_bytes=12 * MIB),
        name="first",
    )(inn, out, near, wz, wy, *arrays)


def half_step(kernel, name, *operands):
    shape = operands[0].shape
    return pl.pallas_call(
        kernel,
        out_shape=jax.ShapeDtypeStruct(shape, jnp.float32),
        in_specs=[VMEM] * len(operands),
        out_specs=VMEM,
        scratch_shapes=work_space(*shape[2:]),
        cost_estimate=CHEAP,
        compiler_params=pltpu.CompilerParams(vmem_limit_bytes=12 * MIB),
        name=name,
    )(*operands)


def finish_kernel(halo, base, coef, wz, out, hi, lo):
    rows = halo.shape[2]
    sign = (1 - 2 * is_flipped(False)).astype(jnp.float32)
    wx = [sign * w for w in mixed_w]
    for f in range(2):
        for j in range(4):
            at_row = pl.ds((f * 4 + j) * rows, rows)
            hi[at_row], lo[at_row] = split(halo[f, j])
    for f in range(2):
        part = pl.ds(f * 4 * rows, 4 * rows)
        dz = dot(hi[part], wz[1]) + dot(lo[part], wz[1])
        for m in range(4):
            hx = zx = None
            for k in range(m + 1, 5):
                j = k - m - 1
                t = float(second_int[k]) * halo[f, j]
                hx = t if hx is None else hx + t
                t = wx[k - 1] * dz[j * rows : (j + 1) * rows]
                zx = t if zx is None else zx + t
            out[f, m] = base[f, m] + (1.0 / SCALE) * (coef[0, m] * hx - coef[2, m] * zx)


def finish(halo, base, coef, wz):
    rows, depth = halo.shape[2:]
    return pl.pallas_call(
        finish_kernel,
        out_shape=jax.ShapeDtypeStruct(halo.shape, jnp.float32),
        in_specs=[VMEM] * 4,
        out_specs=VMEM,
        scratch_shapes=[pltpu.VMEM((8 * rows, depth), jnp.bfloat16)] * 2,
        cost_estimate=CHEAP,
        compiler_params=pltpu.CompilerParams(vmem_limit_bytes=8 * MIB),
        name="finish",
    )(halo, base, coef, wz)


def find_slots(offsets, slots):
    for k in range(NOFF):
        slots[offsets[k]] = k


def slot_of(slots, inner, h):
    return slots[(1 - 2 * is_flipped(inner)) * h + HMAX]


BY_REACH = (-4, 4, -3, 3, -2, 2, -1, 1, 0)


def add_terms(old, new, slot, h, planes, mute, snaps, inner):
    flip = is_flipped(inner)
    rows = old.shape[2]

    def body(i, carry):
        span = pl.ds(pl.multiple_of(i * CHUNK, CHUNK), CHUNK)
        for m in planes:
            total = None
            for half, other, halo in snaps:
                t = at(half, other, halo, 0, m - h)[span] * at(half, other, halo, 1, m + h)[span]
                total = t if total is None else total + t
            local = m + flip * (3 - 2 * m)
            new[slot, local, span] = old[slot, local, span] + mute[natural(m, flip), span] * total
        return carry

    lax.fori_loop(0, rows // CHUNK, body, 0)


def store_planes(buffer, image, slot, first, count, inner, sem):
    flip = is_flipped(inner)
    start = first + flip * (4 - 2 * first - count)
    return pltpu.make_async_copy(
        buffer.at[slot, pl.ds(start, count)], image.at[slot, pl.ds(4 * flip + start, count)], sem
    )


def image_mid_kernel(image_in, offsets, mute, half, other, halo, acc, slots, sem):
    find_slots(offsets, slots)
    near = pl.ds(4 * is_flipped(False), 4)
    slot = [slot_of(slots, False, h) for h in BY_REACH]
    copies = [
        pltpu.make_async_copy(image_in.at[k, near], acc.at[k], sem.at[i])
        for i, k in enumerate(slot)
    ]
    for c in copies:
        c.start()
    for i, h in enumerate(BY_REACH):
        copies[i].wait()
        add_terms(acc, acc, slot[i], h, range(4), mute, [(half, other, halo)], False)


def image_mid(image_in, offsets, mute, half, other, halo):
    shape = (NOFF, 4) + half.shape[2:]
    return pl.pallas_call(
        image_mid_kernel,
        out_shape=jax.ShapeDtypeStruct(shape, jnp.float32),
        in_specs=[HBM, SMEM] + [VMEM] * 4,
        out_specs=VMEM,
        scratch_shapes=[pltpu.SMEM((NOFF,), jnp.int32), pltpu.SemaphoreType.DMA((NOFF,))],
        cost_estimate=CHEAP,
        compiler_params=pltpu.CompilerParams(vmem_limit_bytes=8 * MIB),
        name="image_mid",
    )(image_in, offsets, mute, half, other, halo)


def image_main_kernel(
    image_in, part, offsets, mute, in2, out2, hal2, in4, out4, hal4,
    image, src, rec, acc, done, slots, sem, sems,
):
    find_slots(offsets, slots)
    inner_half = pl.ds(4 * is_flipped(True), 4)
    inner_slot = [slot_of(slots, True, h) for h in BY_REACH]
    outer_slot = [slot_of(slots, False, h) for h in BY_REACH]
    fetches = [
        pltpu.make_async_copy(image_in.at[k, inner_half], acc.at[k], sem.at[i])
        for i, k in enumerate(inner_slot)
    ]
    for c in fetches:
        c.start()
    copies = []
    for inner, field4 in ((True, in4), (False, out4)):
        for f, last in ((0, src), (1, rec)):
            for m in range(4):
                copies.append(
                    pltpu.make_async_copy(
                        field4.at[f, m], last.at[natural(m, is_flipped(inner))], sems.at[len(copies)]
                    )
                )
    for c in copies:
        c.start()
    stores = []
    for i, h in enumerate(BY_REACH):
        reach = abs(h)
        if reach == 4:
            continue
        k = outer_slot[i]
        add_terms(part, done, k, h, range(reach, 4), mute, [(out4, in4, None)], False)
        stores.append(store_planes(done, image, k, reach, 4 - reach, False, sem.at[NOFF + i]))
        stores[-1].start()
    for i, h in enumerate(BY_REACH):
        fetches[i].wait()
        k = inner_slot[i]
        add_terms(acc, acc, k, h, range(4), mute, [(in2, out2, hal2), (in4, out4, hal4)], True)
        stores.append(store_planes(acc, image, k, 0, 4, True, sem.at[i]))
        stores[-1].start()
    for c in copies + stores:
        c.wait()


def image_main(image_in, part, offsets, mute, snap2, snap4):
    shape = snap2[0].shape
    field = jax.ShapeDtypeStruct((8,) + shape[2:], jnp.float32)
    return pl.pallas_call(
        image_main_kernel,
        out_shape=[jax.ShapeDtypeStruct(image_in.shape, jnp.float32), field, field],
        in_specs=[HBM, VMEM, SMEM] + [VMEM] * 7,
        out_specs=[HBM] * 3,
        scratch_shapes=[
            pltpu.VMEM(part.shape, jnp.float32),
            pltpu.VMEM(part.shape, jnp.float32),
            pltpu.SMEM((NOFF,), jnp.int32),
            pltpu.SemaphoreType.DMA((2 * NOFF,)),
            pltpu.SemaphoreType.DMA((16,)),
        ],
        cost_estimate=CHEAP,
        compiler_params=pltpu.CompilerParams(vmem_limit_bytes=8 * MIB),
        name="image_main",
    )(image_in, part, offsets, mute, *snap2, *snap4)


def image_last_kernel(image_old, part, offsets, mute, half, other, halo, image, done, slots, sem):
    del image_old
    find_slots(offsets, slots)
    stores = []
    for i, h in enumerate(BY_REACH[:-1]):
        reach = abs(h)
        k = slot_of(slots, False, h)
        add_terms(part, done, k, h, range(reach), mute, [(half, other, halo)], False)
        stores.append(store_planes(done, image, k, 0, reach, False, sem.at[i]))
        stores[-1].start()
    for c in stores:
        c.wait()


def image_last(image, part, offsets, mute, snap4):
    return pl.pallas_call(
        image_last_kernel,
        out_shape=jax.ShapeDtypeStruct(image.shape, jnp.float32),
        in_specs=[HBM, VMEM, SMEM] + [VMEM] * 4,
        out_specs=HBM,
        scratch_shapes=[
            pltpu.VMEM(part.shape, jnp.float32),
            pltpu.SMEM((NOFF,), jnp.int32),
            pltpu.SemaphoreType.DMA((NOFF,)),
        ],
        input_output_aliases={0: 0},
        cost_estimate=CHEAP,
        compiler_params=pltpu.CompilerParams(vmem_limit_bytes=8 * MIB),
        name="image_last",
    )(image, part, offsets, mute, *snap4)


def across_chips(value, start=1, stride=2):
    count = lax.axis_size("blk")
    pairs = [(i, i + 1) for i in range(start, count - 1, stride)]
    return lax.ppermute(value, "blk", pairs + [(b, a) for a, b in pairs])


def within_chip(value):
    return lax.ppermute(value, "blk", [(i, i ^ 1) for i in range(lax.axis_size("blk"))])


def per_device(
    source_prev,
    source_cur,
    receiver_prev,
    receiver_cur,
    coef_horiz,
    coef_vert,
    coef_mixed,
    live_depth,
    offsets,
    image_in,
):
    source_prev, source_cur = source_prev[0], source_cur[0]
    receiver_prev, receiver_cur = receiver_prev[0], receiver_cur[0]
    coefs = [coef_horiz[0], coef_vert[0], coef_mixed[0]]
    image_in = image_in[:, 0]
    rows, depth = source_cur.shape[1:]
    wz, wy = bands(depth, rows)
    depth_ids = lax.broadcasted_iota(jnp.int32, source_cur.shape, 2)
    mute = (depth_ids < live_depth[0][:, :, None]).astype(jnp.float32)

    out, inn = gather([source_cur, receiver_cur], [(0, False, (0, 1)), (1, True, (0, 1))])
    far = across_chips(out)
    near = within_chip(inn)
    new_inn, base, coef_inn, coef_out = first(
        inn, out, near, wz, wy, [source_prev, receiver_prev] + coefs
    )
    for n in range(STEPS):
        if n > 0:
            base = half_step(base_kernel, "base", out, inn, prev_out, coef_out, wz, wy)
            new_inn = half_step(inner_kernel, "inner", inn, out, near, prev_inn, coef_inn, wz, wy)
        new_out = finish(far, base, coef_out, wz)
        if n == STEPS // 2:
            snap2 = (inn, out, near)
            part = image_mid(image_in, offsets, mute, out, inn, far)
        prev_inn, prev_out, inn, out = inn, out, new_inn, new_out
        near = within_chip(inn)
        far = across_chips(out)
    image, source_last, receiver_last = image_main(
        image_in, part, offsets, mute, snap2, (inn, out, near)
    )
    image = image_last(image, part, offsets, mute, (out, inn, far))
    return (image[:, None], source_last[None], receiver_last[None])


def solution(mesh):
    in_specs = (
        P(("shots", "blk"), None, None, None),
        P(("shots", "blk"), None, None, None),
        P(("shots", "blk"), None, None, None),
        P(("shots", "blk"), None, None, None),
        P("blk", None, None, None),
        P("blk", None, None, None),
        P("blk", None, None, None),
        P("blk", None, None),
        P(),
        P(None, ("shots", "blk"), None, None, None),
    )
    out_specs = (
        P(None, ("shots", "blk"), None, None, None),
        P(("shots", "blk"), None, None, None),
        P(("shots", "blk"), None, None, None),
    )
    return jax.shard_map(
        per_device, mesh=mesh, in_specs=in_specs, out_specs=out_specs, check_vma=False
    )
```

```python
import functools

import jax
import jax.numpy as jnp
import numpy as np
from jax import lax
from jax.experimental import pallas as pl
from jax.experimental.pallas import tpu as pltpu
from jax.sharding import PartitionSpec as P

STEPS = 4
RAD = 4
HMAX = 4
NOFF = 9

second_w = (-205.0 / 72.0, 8.0 / 5.0, -1.0 / 5.0, 8.0 / 315.0, -1.0 / 560.0)
first_w = (4.0 / 5.0, -1.0 / 5.0, 4.0 / 105.0, -1.0 / 280.0)

VMEM = pl.BlockSpec(memory_space=pltpu.VMEM)
SMEM = pl.BlockSpec(memory_space=pltpu.SMEM)
ANY = pl.BlockSpec(memory_space=pl.ANY)
HBM = pl.BlockSpec(memory_space=pltpu.HBM)
MIB = 1 << 20
BIG = pl.CostEstimate(flops=10000000000, transcendentals=0, bytes_accessed=20000000)
CHEAP = pl.CostEstimate(flops=1, transcendentals=0, bytes_accessed=1)


def parity():
    return lax.rem(lax.axis_index("blk"), 2)


def is_flipped(inner):
    odd = parity()
    return 1 - odd if inner else odd


def natural(plane, flipped):
    return plane + flipped * (7 - 2 * plane)


def at(half, other, halo, field, position):
    if position < 0:
        return pick(halo, field, -1 - position)
    if position < 4:
        return pick(half, field, position)
    return pick(other, field, 7 - position)


def pick(fields, field, plane):
    return fields[field].at[plane] if isinstance(fields, tuple) else fields.at[field, plane]


SCALE = 5040
second_int = tuple(round(SCALE * w) for w in second_w)
first_int = tuple(round(840 * w) for w in first_w)
mixed_w = tuple(SCALE / 840 * w for w in first_w)


def bands(depth, rows):
    d = np.arange(depth)[None, :] - np.arange(depth)[:, None]
    r = np.arange(4 * rows)
    dr = np.where(r[None, :] // rows == r[:, None] // rows, r[None, :] - r[:, None], 99)
    dzz, dz = np.zeros(d.shape), np.zeros(d.shape)
    dyy = np.zeros(dr.shape)
    for k in range(1, 5):
        dzz[np.abs(d) == k] = second_int[k]
        dyy[np.abs(dr) == k] = second_int[k]
        dz[d == -k] = first_int[k - 1]
        dz[d == k] = -first_int[k - 1]
    return jnp.asarray(np.stack([dzz, dz]).astype(jnp.bfloat16)), jnp.asarray(dyy.astype(jnp.bfloat16))


def gather_kernel(plan, n_in, *refs):
    ins, outs, sem = refs[:n_in], refs[n_in:-1], refs[-1]
    copies = []
    for out_id, inner, sources in plan:
        flip = is_flipped(inner)
        for i, src in enumerate(sources):
            for m in range(4):
                copies.append(
                    pltpu.make_async_copy(
                        ins[src].at[natural(m, flip)], outs[out_id].at[i, m], sem.at[len(copies)]
                    )
                )
    for c in copies:
        c.start()
    for c in copies:
        c.wait()


def gather(arrays, plan):
    shape = arrays[0].shape[1:]
    arrays = [pltpu.with_memory_space_constraint(a, pltpu.HBM) for a in arrays]
    return pl.pallas_call(
        functools.partial(gather_kernel, plan, len(arrays)),
        out_shape=[jax.ShapeDtypeStruct((len(s), 4) + shape, jnp.float32) for _, _, s in plan],
        in_specs=[HBM] * len(arrays),
        out_specs=[VMEM] * len(plan),
        scratch_shapes=[pltpu.SemaphoreType.DMA((sum(4 * len(s) for _, _, s in plan),))],
        cost_estimate=BIG,
        compiler_params=pltpu.CompilerParams(vmem_limit_bytes=8 * MIB),
        name="gather",
    )(*arrays)


CHUNK = 16
dot = functools.partial(jnp.dot, preferred_element_type=jnp.float32)


def split(value):
    high = value.astype(jnp.bfloat16)
    return high, (value - high.astype(jnp.float32)).astype(jnp.bfloat16)


def advance(inner, half, other, halo, prev, coef, wz, wy, out, v_hi, v_lo, x_hi, x_lo, horiz):
    rows = half.shape[2]
    sign = (1 - 2 * is_flipped(inner)).astype(jnp.float32)
    wx = [sign * w for w in mixed_w]

    for f in range(2):
        for r in range(0, rows, CHUNK):
            span = pl.ds(r, CHUNK)
            low = 0 if halo is None else -4
            line = {q: at(half, other, halo, f, q)[span] for q in range(low, 8)}
            for m in range(4):
                center = line[m]
                hx = (2.0 * SCALE * second_w[0]) * center
                dx = None
                for k in range(1, 5):
                    up = line[m + k]
                    if m - k in line:
                        both, t = up + line[m - k], up - line[m - k]
                    else:
                        both, t = up, up
                    hx = hx + float(second_int[k]) * both
                    t = wx[k - 1] * t
                    dx = t if dx is None else dx + t
                horiz[f, m, span] = hx
                at_row = pl.ds((f * 4 + m) * rows + r, CHUNK)
                v_hi[at_row], v_lo[at_row] = split(center)
                x_hi[at_row], x_lo[at_row] = split(dx)
        part = pl.ds(f * 4 * rows, 4 * rows)
        vh, vl, xh, xl = v_hi[part], v_lo[part], x_hi[part], x_lo[part]
        zz = dot(vh, wz[0]) + dot(vl, wz[0])
        zx = dot(xh, wz[1]) + dot(xl, wz[1])
        yy = dot(wy[...], vh) + dot(wy[...], vl)
        for m in range(4):
            cut = slice(m * rows, (m + 1) * rows)
            center = half[f, m]
            out[f, m] = (
                2.0 * center
                - prev[f, m]
                + (1.0 / SCALE)
                * (
                    coef[0, m] * (horiz[f, m] + yy[cut])
                    + coef[1, m] * (zz[cut] + (SCALE * second_w[0]) * center)
                    + coef[2, m] * zx[cut]
                )
            )


def inner_kernel(inn, out, near, prev_inn, coef_inn, wz, wy, new_inn, *scratch):
    advance(True, inn, out, near, prev_inn, coef_inn, wz, wy, new_inn, *scratch)


def base_kernel(out, inn, prev_out, coef_out, wz, wy, base, *scratch):
    advance(False, out, inn, None, prev_out, coef_out, wz, wy, base, *scratch)


def first_kernel(
    out, inn, wz, wy, source_prev, receiver_prev, coef_a, coef_b, coef_c,
    base, coef_inn, coef_out, prev_inn, prev_out, sem, *scratch
):
    coefs = (coef_a, coef_b, coef_c)
    prevs = (source_prev, receiver_prev)
    copies = []
    for inner, pairs in (
        (False, [(c, coef_out.at[i]) for i, c in enumerate(coefs)]),
        (False, [(c, prev_out.at[i]) for i, c in enumerate(prevs)]),
        (True, [(c, coef_inn.at[i]) for i, c in enumerate(coefs)]),
        (True, [(c, prev_inn.at[i]) for i, c in enumerate(prevs)]),
    ):
        for source, target in pairs:
            for m in range(4):
                copies.append(
                    pltpu.make_async_copy(
                        source.at[natural(m, is_flipped(inner))], target.at[m], sem.at[len(copies)]
                    )
                )
    for c in copies:
        c.start()
    for c in copies[:20]:
        c.wait()
    advance(False, out, inn, None, prev_out, coef_out, wz, wy, base, *scratch)
    for c in copies[20:]:
        c.wait()


def work_space(rows, depth):
    flat = pltpu.VMEM((8 * rows, depth), jnp.bfloat16)
    return [flat] * 4 + [pltpu.VMEM((2, 4, rows, depth), jnp.float32)]


def first(out, inn, wz, wy, arrays):
    rows, depth = out.shape[2:]
    arrays = [pltpu.with_memory_space_constraint(a, pltpu.HBM) for a in arrays]
    pair = jax.ShapeDtypeStruct((2, 4, rows, depth), jnp.float32)
    three = jax.ShapeDtypeStruct((3, 4, rows, depth), jnp.float32)
    half = pltpu.VMEM((2, 4, rows, depth), jnp.float32)
    return pl.pallas_call(
        first_kernel,
        out_shape=[pair, three, three, pair],
        in_specs=[VMEM] * 4 + [HBM] * 5,
        out_specs=[VMEM] * 4,
        scratch_shapes=[half, pltpu.SemaphoreType.DMA((40,))] + work_space(rows, depth),
        cost_estimate=BIG,
        compiler_params=pltpu.CompilerParams(vmem_limit_bytes=12 * MIB),
        name="first",
    )(out, inn, wz, wy, *arrays)


def half_step(kernel, name, *operands):
    shape = operands[0].shape
    return pl.pallas_call(
        kernel,
        out_shape=jax.ShapeDtypeStruct(shape, jnp.float32),
        in_specs=[VMEM] * len(operands),
        out_specs=VMEM,
        scratch_shapes=work_space(*shape[2:]),
        cost_estimate=CHEAP,
        compiler_params=pltpu.CompilerParams(vmem_limit_bytes=12 * MIB),
        name=name,
    )(*operands)


def finish_kernel(halo, base, coef, wz, out, hi, lo):
    rows = halo.shape[2]
    sign = (1 - 2 * is_flipped(False)).astype(jnp.float32)
    wx = [sign * w for w in mixed_w]
    for f in range(2):
        for j in range(4):
            at_row = pl.ds((f * 4 + j) * rows, rows)
            hi[at_row], lo[at_row] = split(halo[f, j])
    for f in range(2):
        part = pl.ds(f * 4 * rows, 4 * rows)
        dz = dot(hi[part], wz[1]) + dot(lo[part], wz[1])
        for m in range(4):
            hx = zx = None
            for k in range(m + 1, 5):
                j = k - m - 1
                t = float(second_int[k]) * halo[f, j]
                hx = t if hx is None else hx + t
                t = wx[k - 1] * dz[j * rows : (j + 1) * rows]
                zx = t if zx is None else zx + t
            out[f, m] = base[f, m] + (1.0 / SCALE) * (coef[0, m] * hx - coef[2, m] * zx)


def finish(halo, base, coef, wz):
    rows, depth = halo.shape[2:]
    return pl.pallas_call(
        finish_kernel,
        out_shape=jax.ShapeDtypeStruct(halo.shape, jnp.float32),
        in_specs=[VMEM] * 4,
        out_specs=VMEM,
        scratch_shapes=[pltpu.VMEM((8 * rows, depth), jnp.bfloat16)] * 2,
        cost_estimate=CHEAP,
        compiler_params=pltpu.CompilerParams(vmem_limit_bytes=8 * MIB),
        name="finish",
    )(halo, base, coef, wz)


def find_slots(offsets, slots):
    for k in range(NOFF):
        slots[offsets[k]] = k


def slot_of(slots, inner, h):
    return slots[(1 - 2 * is_flipped(inner)) * h + HMAX]


BY_REACH = (-4, 4, -3, 3, -2, 2, -1, 1, 0)


def add_terms(old, new, slot, h, planes, mute, snaps, inner):
    flip = is_flipped(inner)
    rows = old.shape[2]

    def body(i, carry):
        span = pl.ds(pl.multiple_of(i * CHUNK, CHUNK), CHUNK)
        for m in planes:
            total = None
            for half, other, halo in snaps:
                t = at(half, other, halo, 0, m - h)[span] * at(half, other, halo, 1, m + h)[span]
                total = t if total is None else total + t
            local = m + flip * (3 - 2 * m)
            new[slot, local, span] = old[slot, local, span] + mute[natural(m, flip), span] * total
        return carry

    lax.fori_loop(0, rows // CHUNK, body, 0)


def store_planes(buffer, image, slot, first, count, inner, sem):
    flip = is_flipped(inner)
    start = first + flip * (4 - 2 * first - count)
    return pltpu.make_async_copy(
        buffer.at[slot, pl.ds(start, count)], image.at[slot, pl.ds(4 * flip + start, count)], sem
    )


def image_mid_kernel(image_in, offsets, mute, half, other, halo, acc, slots, sem):
    find_slots(offsets, slots)
    near = pl.ds(4 * is_flipped(False), 4)
    slot = [slot_of(slots, False, h) for h in BY_REACH]
    copies = [
        pltpu.make_async_copy(image_in.at[k, near], acc.at[k], sem.at[i])
        for i, k in enumerate(slot)
    ]
    for c in copies:
        c.start()
    for i, h in enumerate(BY_REACH):
        copies[i].wait()
        add_terms(acc, acc, slot[i], h, range(4), mute, [(half, other, halo)], False)


def image_mid(image_in, offsets, mute, half, other, halo):
    shape = (NOFF, 4) + half.shape[2:]
    return pl.pallas_call(
        image_mid_kernel,
        out_shape=jax.ShapeDtypeStruct(shape, jnp.float32),
        in_specs=[HBM, SMEM] + [VMEM] * 4,
        out_specs=VMEM,
        scratch_shapes=[pltpu.SMEM((NOFF,), jnp.int32), pltpu.SemaphoreType.DMA((NOFF,))],
        cost_estimate=CHEAP,
        compiler_params=pltpu.CompilerParams(vmem_limit_bytes=8 * MIB),
        name="image_mid",
    )(image_in, offsets, mute, half, other, halo)


def image_main_kernel(
    image_in, part, offsets, mute, in2, out2, hal2, in4, out4, hal4,
    image, src, rec, acc, done, slots, sem, sems,
):
    find_slots(offsets, slots)
    inner_half = pl.ds(4 * is_flipped(True), 4)
    inner_slot = [slot_of(slots, True, h) for h in BY_REACH]
    outer_slot = [slot_of(slots, False, h) for h in BY_REACH]
    fetches = [
        pltpu.make_async_copy(image_in.at[k, inner_half], acc.at[k], sem.at[i])
        for i, k in enumerate(inner_slot)
    ]
    for c in fetches:
        c.start()
    copies = []
    for inner, field4 in ((True, in4), (False, out4)):
        for f, last in ((0, src), (1, rec)):
            for m in range(4):
                copies.append(
                    pltpu.make_async_copy(
                        field4.at[f, m], last.at[natural(m, is_flipped(inner))], sems.at[len(copies)]
                    )
                )
    for c in copies:
        c.start()
    stores = []
    for i, h in enumerate(BY_REACH):
        reach = abs(h)
        if reach == 4:
            continue
        k = outer_slot[i]
        add_terms(part, done, k, h, range(reach, 4), mute, [(out4, in4, None)], False)
        stores.append(store_planes(done, image, k, reach, 4 - reach, False, sem.at[NOFF + i]))
        stores[-1].start()
    for i, h in enumerate(BY_REACH):
        fetches[i].wait()
        k = inner_slot[i]
        add_terms(acc, acc, k, h, range(4), mute, [(in2, out2, hal2), (in4, out4, hal4)], True)
        stores.append(store_planes(acc, image, k, 0, 4, True, sem.at[i]))
        stores[-1].start()
    for c in copies + stores:
        c.wait()


def image_main(image_in, part, offsets, mute, snap2, snap4):
    shape = snap2[0].shape
    field = jax.ShapeDtypeStruct((8,) + shape[2:], jnp.float32)
    return pl.pallas_call(
        image_main_kernel,
        out_shape=[jax.ShapeDtypeStruct(image_in.shape, jnp.float32), field, field],
        in_specs=[HBM, VMEM, SMEM] + [VMEM] * 7,
        out_specs=[HBM] * 3,
        scratch_shapes=[
            pltpu.VMEM(part.shape, jnp.float32),
            pltpu.VMEM(part.shape, jnp.float32),
            pltpu.SMEM((NOFF,), jnp.int32),
            pltpu.SemaphoreType.DMA((2 * NOFF,)),
            pltpu.SemaphoreType.DMA((16,)),
        ],
        cost_estimate=CHEAP,
        compiler_params=pltpu.CompilerParams(vmem_limit_bytes=8 * MIB),
        name="image_main",
    )(image_in, part, offsets, mute, *snap2, *snap4)


def image_last_kernel(image_old, part, offsets, mute, half, other, halo, image, done, slots, sem):
    del image_old
    find_slots(offsets, slots)
    stores = []
    for i, h in enumerate(BY_REACH[:-1]):
        reach = abs(h)
        k = slot_of(slots, False, h)
        add_terms(part, done, k, h, range(reach), mute, [(half, other, halo)], False)
        stores.append(store_planes(done, image, k, 0, reach, False, sem.at[i]))
        stores[-1].start()
    for c in stores:
        c.wait()


def image_last(image, part, offsets, mute, snap4):
    return pl.pallas_call(
        image_last_kernel,
        out_shape=jax.ShapeDtypeStruct(image.shape, jnp.float32),
        in_specs=[HBM, VMEM, SMEM] + [VMEM] * 4,
        out_specs=HBM,
        scratch_shapes=[
            pltpu.VMEM(part.shape, jnp.float32),
            pltpu.SMEM((NOFF,), jnp.int32),
            pltpu.SemaphoreType.DMA((NOFF,)),
        ],
        input_output_aliases={0: 0},
        cost_estimate=CHEAP,
        compiler_params=pltpu.CompilerParams(vmem_limit_bytes=8 * MIB),
        name="image_last",
    )(image, part, offsets, mute, *snap4)


def across_chips(value, start=1, stride=2):
    count = lax.axis_size("blk")
    pairs = [(i, i + 1) for i in range(start, count - 1, stride)]
    return lax.ppermute(value, "blk", pairs + [(b, a) for a, b in pairs])


def within_chip(value):
    return lax.ppermute(value, "blk", [(i, i ^ 1) for i in range(lax.axis_size("blk"))])


def per_device(
    source_prev,
    source_cur,
    receiver_prev,
    receiver_cur,
    coef_horiz,
    coef_vert,
    coef_mixed,
    live_depth,
    offsets,
    image_in,
):
    source_prev, source_cur = source_prev[0], source_cur[0]
    receiver_prev, receiver_cur = receiver_prev[0], receiver_cur[0]
    coefs = [coef_horiz[0], coef_vert[0], coef_mixed[0]]
    image_in = image_in[:, 0]
    rows, depth = source_cur.shape[1:]
    wz, wy = bands(depth, rows)
    depth_ids = lax.broadcasted_iota(jnp.int32, source_cur.shape, 2)
    mute = (depth_ids < live_depth[0][:, :, None]).astype(jnp.float32)

    (out,) = gather([source_cur, receiver_cur], [(0, False, (0, 1))])
    far = across_chips(out)
    (inn,) = gather([source_cur, receiver_cur], [(0, True, (0, 1))])
    near = within_chip(inn)
    base, coef_inn, coef_out, prev_inn = first(
        out, inn, wz, wy, [source_prev, receiver_prev] + coefs
    )
    for n in range(STEPS):
        if n > 0:
            base = half_step(base_kernel, "base", out, inn, prev_out, coef_out, wz, wy)
        new_inn = half_step(inner_kernel, "inner", inn, out, near, prev_inn, coef_inn, wz, wy)
        new_out = finish(far, base, coef_out, wz)
        if n == STEPS // 2:
            snap2 = (inn, out, near)
            part = image_mid(image_in, offsets, mute, out, inn, far)
        prev_inn, prev_out, inn, out = inn, out, new_inn, new_out
        near = within_chip(inn)
        far = across_chips(out)
    image, source_last, receiver_last = image_main(
        image_in, part, offsets, mute, snap2, (inn, out, near)
    )
    image = image_last(image, part, offsets, mute, (out, inn, far))
    return (image[:, None], source_last[None], receiver_last[None])


def solution(mesh):
    in_specs = (
        P(("shots", "blk"), None, None, None),
        P(("shots", "blk"), None, None, None),
        P(("shots", "blk"), None, None, None),
        P(("shots", "blk"), None, None, None),
        P("blk", None, None, None),
        P("blk", None, None, None),
        P("blk", None, None, None),
        P("blk", None, None),
        P(),
        P(None, ("shots", "blk"), None, None, None),
    )
    out_specs = (
        P(None, ("shots", "blk"), None, None, None),
        P(("shots", "blk"), None, None, None),
        P(("shots", "blk"), None, None, None),
    )
    return jax.shard_map(
        per_device, mesh=mesh, in_specs=in_specs, out_specs=out_specs, check_vma=False
    )
```

```python
import functools

import jax
import jax.numpy as jnp
import numpy as np
from jax import lax
from jax.experimental import pallas as pl
from jax.experimental.pallas import tpu as pltpu
from jax.sharding import PartitionSpec as P

STEPS = 4
RAD = 4
HMAX = 4
NOFF = 9

second_w = (-205.0 / 72.0, 8.0 / 5.0, -1.0 / 5.0, 8.0 / 315.0, -1.0 / 560.0)
first_w = (4.0 / 5.0, -1.0 / 5.0, 4.0 / 105.0, -1.0 / 280.0)

VMEM = pl.BlockSpec(memory_space=pltpu.VMEM)
SMEM = pl.BlockSpec(memory_space=pltpu.SMEM)
ANY = pl.BlockSpec(memory_space=pl.ANY)
HBM = pl.BlockSpec(memory_space=pltpu.HBM)
MIB = 1 << 20
BIG = pl.CostEstimate(flops=10000000000, transcendentals=0, bytes_accessed=20000000)
CHEAP = pl.CostEstimate(flops=1, transcendentals=0, bytes_accessed=1)


def parity():
    return lax.rem(lax.axis_index("blk"), 2)


def is_flipped(inner):
    odd = parity()
    return 1 - odd if inner else odd


def natural(plane, flipped):
    return plane + flipped * (7 - 2 * plane)


def at(half, other, halo, field, position):
    if position < 0:
        return pick(halo, field, -1 - position)
    if position < 4:
        return pick(half, field, position)
    return pick(other, field, 7 - position)


def pick(fields, field, plane):
    return fields[field].at[plane] if isinstance(fields, tuple) else fields.at[field, plane]


SCALE = 5040
second_int = tuple(round(SCALE * w) for w in second_w)
first_int = tuple(round(840 * w) for w in first_w)
mixed_w = tuple(SCALE / 840 * w for w in first_w)


def bands(depth, rows):
    d = np.arange(depth)[None, :] - np.arange(depth)[:, None]
    r = np.arange(4 * rows)
    dr = np.where(r[None, :] // rows == r[:, None] // rows, r[None, :] - r[:, None], 99)
    dzz, dz = np.zeros(d.shape), np.zeros(d.shape)
    dyy = np.zeros(dr.shape)
    for k in range(1, 5):
        dzz[np.abs(d) == k] = second_int[k]
        dyy[np.abs(dr) == k] = second_int[k]
        dz[d == -k] = first_int[k - 1]
        dz[d == k] = -first_int[k - 1]
    return jnp.asarray(np.stack([dzz, dz]).astype(jnp.bfloat16)), jnp.asarray(dyy.astype(jnp.bfloat16))


def gather_kernel(plan, n_in, *refs):
    ins, outs, sem = refs[:n_in], refs[n_in:-1], refs[-1]
    copies = []
    for out_id, inner, sources in plan:
        flip = is_flipped(inner)
        for i, src in enumerate(sources):
            for m in range(4):
                copies.append(
                    pltpu.make_async_copy(
                        ins[src].at[natural(m, flip)], outs[out_id].at[i, m], sem.at[len(copies)]
                    )
                )
    for c in copies:
        c.start()
    for c in copies:
        c.wait()


def gather(arrays, plan):
    shape = arrays[0].shape[1:]
    arrays = [pltpu.with_memory_space_constraint(a, pltpu.HBM) for a in arrays]
    return pl.pallas_call(
        functools.partial(gather_kernel, plan, len(arrays)),
        out_shape=[jax.ShapeDtypeStruct((len(s), 4) + shape, jnp.float32) for _, _, s in plan],
        in_specs=[HBM] * len(arrays),
        out_specs=[VMEM] * len(plan),
        scratch_shapes=[pltpu.SemaphoreType.DMA((sum(4 * len(s) for _, _, s in plan),))],
        cost_estimate=BIG,
        compiler_params=pltpu.CompilerParams(vmem_limit_bytes=8 * MIB),
        name="gather",
    )(*arrays)


CHUNK = 16
dot = functools.partial(jnp.dot, preferred_element_type=jnp.float32)


def split(value):
    high = value.astype(jnp.bfloat16)
    return high, (value - high.astype(jnp.float32)).astype(jnp.bfloat16)


def advance(inner, half, other, halo, prev, coef, wz, wy, out, v_hi, v_lo, x_hi, x_lo, horiz):
    rows = half.shape[2]
    sign = (1 - 2 * is_flipped(inner)).astype(jnp.float32)
    wx = [sign * w for w in mixed_w]

    for f in range(2):
        for r in range(0, rows, CHUNK):
            span = pl.ds(r, CHUNK)
            low = 0 if halo is None else -4
            line = {q: at(half, other, halo, f, q)[span] for q in range(low, 8)}
            for m in range(4):
                center = line[m]
                hx = (2.0 * SCALE * second_w[0]) * center
                dx = None
                for k in range(1, 5):
                    up = line[m + k]
                    if m - k in line:
                        both, t = up + line[m - k], up - line[m - k]
                    else:
                        both, t = up, up
                    hx = hx + float(second_int[k]) * both
                    t = wx[k - 1] * t
                    dx = t if dx is None else dx + t
                horiz[f, m, span] = hx
                at_row = pl.ds((f * 4 + m) * rows + r, CHUNK)
                v_hi[at_row], v_lo[at_row] = split(center)
                x_hi[at_row], x_lo[at_row] = split(dx)
        part = pl.ds(f * 4 * rows, 4 * rows)
        vh, vl, xh, xl = v_hi[part], v_lo[part], x_hi[part], x_lo[part]
        zz = dot(vh, wz[0]) + dot(vl, wz[0])
        zx = dot(xh, wz[1]) + dot(xl, wz[1])
        yy = dot(wy[...], vh) + dot(wy[...], vl)
        for m in range(4):
            cut = slice(m * rows, (m + 1) * rows)
            center = half[f, m]
            out[f, m] = (
                2.0 * center
                - prev[f, m]
                + (1.0 / SCALE)
                * (
                    coef[0, m] * (horiz[f, m] + yy[cut])
                    + coef[1, m] * (zz[cut] + (SCALE * second_w[0]) * center)
                    + coef[2, m] * zx[cut]
                )
            )


def inner_kernel(inn, out, near, prev_inn, coef_inn, wz, wy, new_inn, *scratch):
    advance(True, inn, out, near, prev_inn, coef_inn, wz, wy, new_inn, *scratch)


def base_kernel(out, inn, prev_out, coef_out, wz, wy, base, *scratch):
    advance(False, out, inn, None, prev_out, coef_out, wz, wy, base, *scratch)


def first_kernel(
    out, inn, wz, wy, source_prev, receiver_prev, coef_a, coef_b, coef_c,
    base, coef_inn, coef_out, prev_inn, prev_out, sem, *scratch
):
    coefs = (coef_a, coef_b, coef_c)
    prevs = (source_prev, receiver_prev)
    copies = []
    for inner, pairs in (
        (False, [(c, coef_out.at[i]) for i, c in enumerate(coefs)]),
        (False, [(c, prev_out.at[i]) for i, c in enumerate(prevs)]),
        (True, [(c, coef_inn.at[i]) for i, c in enumerate(coefs)]),
        (True, [(c, prev_inn.at[i]) for i, c in enumerate(prevs)]),
    ):
        for source, target in pairs:
            for m in range(4):
                copies.append(
                    pltpu.make_async_copy(
                        source.at[natural(m, is_flipped(inner))], target.at[m], sem.at[len(copies)]
                    )
                )
    for c in copies:
        c.start()
    for c in copies[:20]:
        c.wait()
    advance(False, out, inn, None, prev_out, coef_out, wz, wy, base, *scratch)
    for c in copies[20:]:
        c.wait()


def work_space(rows, depth):
    flat = pltpu.VMEM((8 * rows, depth), jnp.bfloat16)
    return [flat] * 4 + [pltpu.VMEM((2, 4, rows, depth), jnp.float32)]


def first(out, inn, wz, wy, arrays):
    rows, depth = out.shape[2:]
    arrays = [pltpu.with_memory_space_constraint(a, pltpu.HBM) for a in arrays]
    pair = jax.ShapeDtypeStruct((2, 4, rows, depth), jnp.float32)
    three = jax.ShapeDtypeStruct((3, 4, rows, depth), jnp.float32)
    half = pltpu.VMEM((2, 4, rows, depth), jnp.float32)
    return pl.pallas_call(
        first_kernel,
        out_shape=[pair, three, three, pair],
        in_specs=[VMEM] * 4 + [HBM] * 5,
        out_specs=[VMEM] * 4,
        scratch_shapes=[half, pltpu.SemaphoreType.DMA((40,))] + work_space(rows, depth),
        cost_estimate=BIG,
        compiler_params=pltpu.CompilerParams(vmem_limit_bytes=12 * MIB),
        name="first",
    )(out, inn, wz, wy, *arrays)


def half_step(kernel, name, *operands):
    shape = operands[0].shape
    return pl.pallas_call(
        kernel,
        out_shape=jax.ShapeDtypeStruct(shape, jnp.float32),
        in_specs=[VMEM] * len(operands),
        out_specs=VMEM,
        scratch_shapes=work_space(*shape[2:]),
        cost_estimate=CHEAP,
        compiler_params=pltpu.CompilerParams(vmem_limit_bytes=12 * MIB),
        name=name,
    )(*operands)


def finish_kernel(halo, base, coef, wz, out, hi, lo):
    rows = halo.shape[2]
    sign = (1 - 2 * is_flipped(False)).astype(jnp.float32)
    wx = [sign * w for w in mixed_w]
    for f in range(2):
        for j in range(4):
            at_row = pl.ds((f * 4 + j) * rows, rows)
            hi[at_row], lo[at_row] = split(halo[f, j])
    for f in range(2):
        part = pl.ds(f * 4 * rows, 4 * rows)
        dz = dot(hi[part], wz[1]) + dot(lo[part], wz[1])
        for m in range(4):
            hx = zx = None
            for k in range(m + 1, 5):
                j = k - m - 1
                t = float(second_int[k]) * halo[f, j]
                hx = t if hx is None else hx + t
                t = wx[k - 1] * dz[j * rows : (j + 1) * rows]
                zx = t if zx is None else zx + t
            out[f, m] = base[f, m] + (1.0 / SCALE) * (coef[0, m] * hx - coef[2, m] * zx)


def finish(halo, base, coef, wz):
    rows, depth = halo.shape[2:]
    return pl.pallas_call(
        finish_kernel,
        out_shape=jax.ShapeDtypeStruct(halo.shape, jnp.float32),
        in_specs=[VMEM] * 4,
        out_specs=VMEM,
        scratch_shapes=[pltpu.VMEM((8 * rows, depth), jnp.bfloat16)] * 2,
        cost_estimate=CHEAP,
        compiler_params=pltpu.CompilerParams(vmem_limit_bytes=8 * MIB),
        name="finish",
    )(halo, base, coef, wz)


def find_slots(offsets, slots):
    for k in range(NOFF):
        slots[offsets[k]] = k


def slot_of(slots, inner, h):
    return slots[(1 - 2 * is_flipped(inner)) * h + HMAX]


BY_REACH = (-4, 4, -3, 3, -2, 2, -1, 1, 0)


def add_terms(old, new, slots, planes, mute, snaps, inner):
    flip = is_flipped(inner)
    rows = old.shape[2]
    chunk = CHUNK
    while chunk < rows and 2 * chunk * len(planes) * len(slots) <= 128:
        chunk *= 2

    def body(i, carry):
        span = pl.ds(pl.multiple_of(i * chunk, chunk), chunk)
        for m in planes:
            local = m + flip * (3 - 2 * m)
            mask = mute[natural(m, flip), span]
            for h, slot in slots.items():
                total = None
                for half, other, halo in snaps:
                    t = at(half, other, halo, 0, m - h)[span] * at(half, other, halo, 1, m + h)[span]
                    total = t if total is None else total + t
                new[slot, local, span] = old[slot, local, span] + mask * total
        return carry

    lax.fori_loop(0, rows // chunk, body, 0)


def store_planes(buffer, image, slot, first, count, inner, sem):
    flip = is_flipped(inner)
    start = first + flip * (4 - 2 * first - count)
    return pltpu.make_async_copy(
        buffer.at[slot, pl.ds(start, count)], image.at[slot, pl.ds(4 * flip + start, count)], sem
    )


def image_mid_kernel(image_in, offsets, mute, half, other, halo, acc, slots, sem):
    find_slots(offsets, slots)
    near = pl.ds(4 * is_flipped(False), 4)
    slot = [slot_of(slots, False, h) for h in BY_REACH]
    copies = [
        pltpu.make_async_copy(image_in.at[k, near], acc.at[k], sem.at[i])
        for i, k in enumerate(slot)
    ]
    for c in copies:
        c.start()
    for i, h in enumerate(BY_REACH):
        copies[i].wait()
        add_terms(acc, acc, {h: slot[i]}, range(4), mute, [(half, other, halo)], False)


def image_mid(image_in, offsets, mute, half, other, halo):
    shape = (NOFF, 4) + half.shape[2:]
    return pl.pallas_call(
        image_mid_kernel,
        out_shape=jax.ShapeDtypeStruct(shape, jnp.float32),
        in_specs=[HBM, SMEM] + [VMEM] * 4,
        out_specs=VMEM,
        scratch_shapes=[pltpu.SMEM((NOFF,), jnp.int32), pltpu.SemaphoreType.DMA((NOFF,))],
        cost_estimate=CHEAP,
        compiler_params=pltpu.CompilerParams(vmem_limit_bytes=8 * MIB),
        name="image_mid",
    )(image_in, offsets, mute, half, other, halo)


def image_main_kernel(
    image_in, part, offsets, mute, in2, out2, hal2, in4, out4, hal4,
    image, src, rec, table, acc, done, slots, sem, sems,
):
    find_slots(offsets, slots)
    inner_half = pl.ds(4 * is_flipped(True), 4)
    inner_slot = [slot_of(slots, True, h) for h in BY_REACH]
    outer_slot = [slot_of(slots, False, h) for h in BY_REACH]
    for h, k in zip(BY_REACH, outer_slot):
        table[pl.ds(h + HMAX, 1)] = jnp.full((1, table.shape[1]), k, jnp.int32)
    fetches = [
        pltpu.make_async_copy(image_in.at[k, inner_half], acc.at[k], sem.at[i])
        for i, k in enumerate(inner_slot)
    ]
    for c in fetches:
        c.start()
    copies = []
    for inner, field4 in ((True, in4), (False, out4)):
        for f, last in ((0, src), (1, rec)):
            for m in range(4):
                copies.append(
                    pltpu.make_async_copy(
                        field4.at[f, m], last.at[natural(m, is_flipped(inner))], sems.at[len(copies)]
                    )
                )
    for c in copies:
        c.start()
    stores = []
    for i, h in enumerate(BY_REACH):
        reach = abs(h)
        if reach == 4:
            continue
        k = outer_slot[i]
        add_terms(part, done, {h: k}, range(reach, 4), mute, [(out4, in4, None)], False)
        stores.append(store_planes(done, image, k, reach, 4 - reach, False, sem.at[NOFF + i]))
        stores[-1].start()
    for i, h in enumerate(BY_REACH):
        fetches[i].wait()
        k = inner_slot[i]
        add_terms(acc, acc, {h: k}, range(4), mute, [(in2, out2, hal2), (in4, out4, hal4)], True)
        stores.append(store_planes(acc, image, k, 0, 4, True, sem.at[i]))
        stores[-1].start()
    for c in copies + stores:
        c.wait()


def image_main(image_in, part, offsets, mute, snap2, snap4):
    shape = snap2[0].shape
    field = jax.ShapeDtypeStruct((8,) + shape[2:], jnp.float32)
    return pl.pallas_call(
        image_main_kernel,
        out_shape=[
            jax.ShapeDtypeStruct(image_in.shape, jnp.float32), field, field,
            jax.ShapeDtypeStruct((NOFF, 128), jnp.int32),
        ],
        in_specs=[HBM, VMEM, SMEM] + [VMEM] * 7,
        out_specs=[HBM] * 3 + [VMEM],
        scratch_shapes=[
            pltpu.VMEM(part.shape, jnp.float32),
            pltpu.VMEM(part.shape, jnp.float32),
            pltpu.SMEM((NOFF,), jnp.int32),
            pltpu.SemaphoreType.DMA((2 * NOFF,)),
            pltpu.SemaphoreType.DMA((16,)),
        ],
        cost_estimate=CHEAP,
        compiler_params=pltpu.CompilerParams(vmem_limit_bytes=8 * MIB),
        name="image_main",
    )(image_in, part, offsets, mute, *snap2, *snap4)


def image_last_kernel(image_old, part, table, mute, half, other, halo, image, done, sem):
    del image_old
    stores = []
    for reach in range(HMAX, 0, -1):
        pair = {h: table[h + HMAX, 0] for h in (-reach, reach)}
        add_terms(part, done, pair, range(reach), mute, [(half, other, halo)], False)
        for k in pair.values():
            stores.append(store_planes(done, image, k, 0, reach, False, sem.at[len(stores)]))
            stores[-1].start()
    for c in stores:
        c.wait()


def image_last(image, part, table, mute, snap4):
    return pl.pallas_call(
        image_last_kernel,
        out_shape=jax.ShapeDtypeStruct(image.shape, jnp.float32),
        in_specs=[HBM] + [VMEM] * 6,
        out_specs=HBM,
        scratch_shapes=[
            pltpu.VMEM(part.shape, jnp.float32),
            pltpu.SemaphoreType.DMA((NOFF,)),
        ],
        input_output_aliases={0: 0},
        cost_estimate=CHEAP,
        compiler_params=pltpu.CompilerParams(vmem_limit_bytes=8 * MIB),
        name="image_last",
    )(image, part, table, mute, *snap4)


def across_chips(value, start=1, stride=2):
    count = lax.axis_size("blk")
    pairs = [(i, i + 1) for i in range(start, count - 1, stride)]
    return lax.ppermute(value, "blk", pairs + [(b, a) for a, b in pairs])


def within_chip(value):
    return lax.ppermute(value, "blk", [(i, i ^ 1) for i in range(lax.axis_size("blk"))])


def per_device(
    source_prev,
    source_cur,
    receiver_prev,
    receiver_cur,
    coef_horiz,
    coef_vert,
    coef_mixed,
    live_depth,
    offsets,
    image_in,
):
    source_prev, source_cur = source_prev[0], source_cur[0]
    receiver_prev, receiver_cur = receiver_prev[0], receiver_cur[0]
    coefs = [coef_horiz[0], coef_vert[0], coef_mixed[0]]
    image_in = image_in[:, 0]
    rows, depth = source_cur.shape[1:]
    wz, wy = bands(depth, rows)
    depth_ids = lax.broadcasted_iota(jnp.int32, source_cur.shape, 2)
    mute = (depth_ids < live_depth[0][:, :, None]).astype(jnp.float32)

    (out,) = gather([source_cur, receiver_cur], [(0, False, (0, 1))])
    far = across_chips(out)
    (inn,) = gather([source_cur, receiver_cur], [(0, True, (0, 1))])
    near = within_chip(inn)
    base, coef_inn, coef_out, prev_inn = first(
        out, inn, wz, wy, [source_prev, receiver_prev] + coefs
    )
    for n in range(STEPS):
        if n > 0:
            base = half_step(base_kernel, "base", out, inn, prev_out, coef_out, wz, wy)
        new_inn = half_step(inner_kernel, "inner", inn, out, near, prev_inn, coef_inn, wz, wy)
        new_out = finish(far, base, coef_out, wz)
        if n == STEPS // 2:
            snap2 = (inn, out, near)
            part = image_mid(image_in, offsets, mute, out, inn, far)
        prev_inn, prev_out, inn, out = inn, out, new_inn, new_out
        near = within_chip(inn)
        far = across_chips(out)
    image, source_last, receiver_last, table = image_main(
        image_in, part, offsets, mute, snap2, (inn, out, near)
    )
    image = image_last(image, part, table, mute, (out, inn, far))
    return (image[:, None], source_last[None], receiver_last[None])


def solution(mesh):
    in_specs = (
        P(("shots", "blk"), None, None, None),
        P(("shots", "blk"), None, None, None),
        P(("shots", "blk"), None, None, None),
        P(("shots", "blk"), None, None, None),
        P("blk", None, None, None),
        P("blk", None, None, None),
        P("blk", None, None, None),
        P("blk", None, None),
        P(),
        P(None, ("shots", "blk"), None, None, None),
    )
    out_specs = (
        P(None, ("shots", "blk"), None, None, None),
        P(("shots", "blk"), None, None, None),
        P(("shots", "blk"), None, None, None),
    )
    return jax.shard_map(
        per_device, mesh=mesh, in_specs=in_specs, out_specs=out_specs, check_vma=False
    )
```

```python
import functools

import jax
import jax.numpy as jnp
import numpy as np
from jax import lax
from jax.experimental import pallas as pl
from jax.experimental.pallas import tpu as pltpu
from jax.sharding import PartitionSpec as P

STEPS = 4
RAD = 4
HMAX = 4
NOFF = 9

second_w = (-205.0 / 72.0, 8.0 / 5.0, -1.0 / 5.0, 8.0 / 315.0, -1.0 / 560.0)
first_w = (4.0 / 5.0, -1.0 / 5.0, 4.0 / 105.0, -1.0 / 280.0)

VMEM = pl.BlockSpec(memory_space=pltpu.VMEM)
SMEM = pl.BlockSpec(memory_space=pltpu.SMEM)
ANY = pl.BlockSpec(memory_space=pl.ANY)
HBM = pl.BlockSpec(memory_space=pltpu.HBM)
MIB = 1 << 20
BIG = pl.CostEstimate(flops=10000000000, transcendentals=0, bytes_accessed=20000000)
CHEAP = pl.CostEstimate(flops=1, transcendentals=0, bytes_accessed=1)


def parity():
    return lax.rem(lax.axis_index("blk"), 2)


def is_flipped(inner):
    odd = parity()
    return 1 - odd if inner else odd


def natural(plane, flipped):
    return plane + flipped * (7 - 2 * plane)


def at(half, other, halo, field, position):
    if position < 0:
        return pick(halo, field, -1 - position)
    if position < 4:
        return pick(half, field, position)
    return pick(other, field, 7 - position)


def pick(fields, field, plane):
    return fields[field].at[plane] if isinstance(fields, tuple) else fields.at[field, plane]


SCALE = 5040
second_int = tuple(round(SCALE * w) for w in second_w)
first_int = tuple(round(840 * w) for w in first_w)
mixed_w = tuple(SCALE / 840 * w for w in first_w)


def bands(depth, rows):
    d = np.arange(depth)[None, :] - np.arange(depth)[:, None]
    r = np.arange(4 * rows)
    dr = np.where(r[None, :] // rows == r[:, None] // rows, r[None, :] - r[:, None], 99)
    dzz, dz = np.zeros(d.shape), np.zeros(d.shape)
    dyy = np.zeros(dr.shape)
    for k in range(1, 5):
        dzz[np.abs(d) == k] = second_int[k]
        dyy[np.abs(dr) == k] = second_int[k]
        dz[d == -k] = first_int[k - 1]
        dz[d == k] = -first_int[k - 1]
    return jnp.asarray(np.stack([dzz, dz]).astype(jnp.bfloat16)), jnp.asarray(dyy.astype(jnp.bfloat16))


def gather_kernel(plan, n_in, *refs):
    ins, outs, sem = refs[:n_in], refs[n_in:-1], refs[-1]
    copies = []
    for out_id, inner, sources in plan:
        flip = is_flipped(inner)
        for i, src in enumerate(sources):
            for m in range(4):
                copies.append(
                    pltpu.make_async_copy(
                        ins[src].at[natural(m, flip)], outs[out_id].at[i, m], sem.at[len(copies)]
                    )
                )
    for c in copies:
        c.start()
    for c in copies:
        c.wait()


def gather(arrays, plan):
    shape = arrays[0].shape[1:]
    arrays = [pltpu.with_memory_space_constraint(a, pltpu.HBM) for a in arrays]
    return pl.pallas_call(
        functools.partial(gather_kernel, plan, len(arrays)),
        out_shape=[jax.ShapeDtypeStruct((len(s), 4) + shape, jnp.float32) for _, _, s in plan],
        in_specs=[HBM] * len(arrays),
        out_specs=[VMEM] * len(plan),
        scratch_shapes=[pltpu.SemaphoreType.DMA((sum(4 * len(s) for _, _, s in plan),))],
        cost_estimate=BIG,
        compiler_params=pltpu.CompilerParams(vmem_limit_bytes=8 * MIB),
        name="gather",
    )(*arrays)


CHUNK = 16
dot = functools.partial(jnp.dot, preferred_element_type=jnp.float32)


def split(value):
    high = value.astype(jnp.bfloat16)
    return high, (value - high.astype(jnp.float32)).astype(jnp.bfloat16)


def advance(inner, half, other, halo, prev, coef, wz, wy, out, v_hi, v_lo, x_hi, x_lo, horiz):
    rows = half.shape[2]
    sign = (1 - 2 * is_flipped(inner)).astype(jnp.float32)
    wx = [sign * w for w in mixed_w]

    for f in range(2):
        for r in range(0, rows, CHUNK):
            span = pl.ds(r, CHUNK)
            low = 0 if halo is None else -4
            line = {q: at(half, other, halo, f, q)[span] for q in range(low, 8)}
            for m in range(4):
                center = line[m]
                hx = (2.0 * SCALE * second_w[0]) * center
                dx = None
                for k in range(1, 5):
                    up = line[m + k]
                    if m - k in line:
                        both, t = up + line[m - k], up - line[m - k]
                    else:
                        both, t = up, up
                    hx = hx + float(second_int[k]) * both
                    t = wx[k - 1] * t
                    dx = t if dx is None else dx + t
                horiz[f, m, span] = hx
                at_row = pl.ds((f * 4 + m) * rows + r, CHUNK)
                v_hi[at_row], v_lo[at_row] = split(center)
                x_hi[at_row], x_lo[at_row] = split(dx)
        part = pl.ds(f * 4 * rows, 4 * rows)
        vh, vl, xh, xl = v_hi[part], v_lo[part], x_hi[part], x_lo[part]
        zz = dot(vh, wz[0]) + dot(vl, wz[0])
        zx = dot(xh, wz[1]) + dot(xl, wz[1])
        yy = dot(wy[...], vh) + dot(wy[...], vl)
        for m in range(4):
            cut = slice(m * rows, (m + 1) * rows)
            center = half[f, m]
            out[f, m] = (
                2.0 * center
                - prev[f, m]
                + (1.0 / SCALE)
                * (
                    coef[0, m] * (horiz[f, m] + yy[cut])
                    + coef[1, m] * (zz[cut] + (SCALE * second_w[0]) * center)
                    + coef[2, m] * zx[cut]
                )
            )


def inner_kernel(inn, out, near, prev_inn, coef_inn, wz, wy, new_inn, *scratch):
    advance(True, inn, out, near, prev_inn, coef_inn, wz, wy, new_inn, *scratch)


def base_kernel(out, inn, prev_out, coef_out, wz, wy, base, *scratch):
    advance(False, out, inn, None, prev_out, coef_out, wz, wy, base, *scratch)


def first_kernel(
    out, inn, wz, wy, source_prev, receiver_prev, coef_a, coef_b, coef_c,
    base, coef_inn, coef_out, prev_inn, prev_out, sem, *scratch
):
    coefs = (coef_a, coef_b, coef_c)
    prevs = (source_prev, receiver_prev)
    copies = []
    for inner, pairs in (
        (False, [(c, coef_out.at[i]) for i, c in enumerate(coefs)]),
        (False, [(c, prev_out.at[i]) for i, c in enumerate(prevs)]),
        (True, [(c, coef_inn.at[i]) for i, c in enumerate(coefs)]),
        (True, [(c, prev_inn.at[i]) for i, c in enumerate(prevs)]),
    ):
        for source, target in pairs:
            for m in range(4):
                copies.append(
                    pltpu.make_async_copy(
                        source.at[natural(m, is_flipped(inner))], target.at[m], sem.at[len(copies)]
                    )
                )
    for c in copies:
        c.start()
    for c in copies[:20]:
        c.wait()
    advance(False, out, inn, None, prev_out, coef_out, wz, wy, base, *scratch)
    for c in copies[20:]:
        c.wait()


def work_space(rows, depth):
    flat = pltpu.VMEM((8 * rows, depth), jnp.bfloat16)
    return [flat] * 4 + [pltpu.VMEM((2, 4, rows, depth), jnp.float32)]


def first(out, inn, wz, wy, arrays):
    rows, depth = out.shape[2:]
    arrays = [pltpu.with_memory_space_constraint(a, pltpu.HBM) for a in arrays]
    pair = jax.ShapeDtypeStruct((2, 4, rows, depth), jnp.float32)
    three = jax.ShapeDtypeStruct((3, 4, rows, depth), jnp.float32)
    half = pltpu.VMEM((2, 4, rows, depth), jnp.float32)
    return pl.pallas_call(
        first_kernel,
        out_shape=[pair, three, three, pair],
        in_specs=[VMEM] * 4 + [HBM] * 5,
        out_specs=[VMEM] * 4,
        scratch_shapes=[half, pltpu.SemaphoreType.DMA((40,))] + work_space(rows, depth),
        cost_estimate=BIG,
        compiler_params=pltpu.CompilerParams(vmem_limit_bytes=12 * MIB),
        name="first",
    )(out, inn, wz, wy, *arrays)


def half_step(kernel, name, *operands):
    shape = operands[0].shape
    return pl.pallas_call(
        kernel,
        out_shape=jax.ShapeDtypeStruct(shape, jnp.float32),
        in_specs=[VMEM] * len(operands),
        out_specs=VMEM,
        scratch_shapes=work_space(*shape[2:]),
        cost_estimate=CHEAP,
        compiler_params=pltpu.CompilerParams(vmem_limit_bytes=12 * MIB),
        name=name,
    )(*operands)


def finish_kernel(halo, base, coef, wz, out, hi, lo, dz):
    rows = halo.shape[2]
    sign = (1 - 2 * is_flipped(False)).astype(jnp.float32)
    wx = [sign * w / SCALE for w in mixed_w]
    for f in range(2):
        for j in range(4):
            at_row = pl.ds((f * 4 + j) * rows, rows)
            hi[at_row], lo[at_row] = split(halo[f, j])
    dz[...] = dot(hi[...], wz[1]) + dot(lo[...], wz[1])

    for r in range(0, rows, CHUNK):
        span = pl.ds(r, CHUNK)
        for f in range(2):
            h = [halo[f, j, span] for j in range(4)]
            z = [dz[pl.ds((f * 4 + j) * rows + r, CHUNK)] for j in range(4)]
            for m in range(4):
                hx = zx = None
                for k in range(m + 1, 5):
                    t = second_w[k] * h[k - m - 1]
                    hx = t if hx is None else hx + t
                    t = wx[k - 1] * z[k - m - 1]
                    zx = t if zx is None else zx + t
                out[f, m, span] = base[f, m, span] + (coef[0, m, span] * hx - coef[2, m, span] * zx)


def finish(halo, base, coef, wz):
    rows, depth = halo.shape[2:]
    return pl.pallas_call(
        finish_kernel,
        out_shape=jax.ShapeDtypeStruct(halo.shape, jnp.float32),
        in_specs=[VMEM] * 4,
        out_specs=VMEM,
        scratch_shapes=[pltpu.VMEM((8 * rows, depth), jnp.bfloat16)] * 2
        + [pltpu.VMEM((8 * rows, depth), jnp.float32)],
        cost_estimate=CHEAP,
        compiler_params=pltpu.CompilerParams(vmem_limit_bytes=8 * MIB),
        name="finish",
    )(halo, base, coef, wz)


def find_slots(offsets, slots):
    for k in range(NOFF):
        slots[offsets[k]] = k


def slot_of(slots, inner, h):
    return slots[(1 - 2 * is_flipped(inner)) * h + HMAX]


BY_REACH = (-4, 4, -3, 3, -2, 2, -1, 1, 0)


def add_terms(old, new, slots, planes, mute, snaps, inner):
    flip = is_flipped(inner)
    rows = old.shape[2]
    chunk = CHUNK
    while chunk < rows and 2 * chunk * len(planes) * len(slots) <= 128:
        chunk *= 2

    def body(i, carry):
        span = pl.ds(pl.multiple_of(i * chunk, chunk), chunk)
        for m in planes:
            local = m + flip * (3 - 2 * m)
            mask = mute[natural(m, flip), span]
            for h, slot in slots.items():
                total = None
                for half, other, halo in snaps:
                    t = at(half, other, halo, 0, m - h)[span] * at(half, other, halo, 1, m + h)[span]
                    total = t if total is None else total + t
                new[slot, local, span] = old[slot, local, span] + mask * total
        return carry

    lax.fori_loop(0, rows // chunk, body, 0)


def store_planes(buffer, image, slot, first, count, inner, sem):
    flip = is_flipped(inner)
    start = first + flip * (4 - 2 * first - count)
    return pltpu.make_async_copy(
        buffer.at[slot, pl.ds(start, count)], image.at[slot, pl.ds(4 * flip + start, count)], sem
    )


def image_mid_kernel(image_in, offsets, mute, half, other, halo, acc, slots, sem):
    find_slots(offsets, slots)
    near = pl.ds(4 * is_flipped(False), 4)
    slot = [slot_of(slots, False, h) for h in BY_REACH]
    copies = [
        pltpu.make_async_copy(image_in.at[k, near], acc.at[k], sem.at[i])
        for i, k in enumerate(slot)
    ]
    for c in copies:
        c.start()
    for i, h in enumerate(BY_REACH):
        copies[i].wait()
        add_terms(acc, acc, {h: slot[i]}, range(4), mute, [(half, other, halo)], False)


def image_mid(image_in, offsets, mute, half, other, halo):
    shape = (NOFF, 4) + half.shape[2:]
    return pl.pallas_call(
        image_mid_kernel,
        out_shape=jax.ShapeDtypeStruct(shape, jnp.float32),
        in_specs=[HBM, SMEM] + [VMEM] * 4,
        out_specs=VMEM,
        scratch_shapes=[pltpu.SMEM((NOFF,), jnp.int32), pltpu.SemaphoreType.DMA((NOFF,))],
        cost_estimate=CHEAP,
        compiler_params=pltpu.CompilerParams(vmem_limit_bytes=8 * MIB),
        name="image_mid",
    )(image_in, offsets, mute, half, other, halo)


def image_main_kernel(
    image_in, part, offsets, mute, in2, out2, hal2, in4, out4, hal4,
    image, src, rec, table, acc, done, slots, sem, sems,
):
    find_slots(offsets, slots)
    inner_half = pl.ds(4 * is_flipped(True), 4)
    inner_slot = [slot_of(slots, True, h) for h in BY_REACH]
    outer_slot = [slot_of(slots, False, h) for h in BY_REACH]
    for h, k in zip(BY_REACH, outer_slot):
        table[pl.ds(h + HMAX, 1)] = jnp.full((1, table.shape[1]), k, jnp.int32)
    fetches = [
        pltpu.make_async_copy(image_in.at[k, inner_half], acc.at[k], sem.at[i])
        for i, k in enumerate(inner_slot)
    ]
    for c in fetches:
        c.start()
    copies = []
    for inner, field4 in ((True, in4), (False, out4)):
        for f, last in ((0, src), (1, rec)):
            for m in range(4):
                copies.append(
                    pltpu.make_async_copy(
                        field4.at[f, m], last.at[natural(m, is_flipped(inner))], sems.at[len(copies)]
                    )
                )
    for c in copies:
        c.start()
    stores = []
    for i, h in enumerate(BY_REACH):
        reach = abs(h)
        if reach == 4:
            continue
        k = outer_slot[i]
        add_terms(part, done, {h: k}, range(reach, 4), mute, [(out4, in4, None)], False)
        stores.append(store_planes(done, image, k, reach, 4 - reach, False, sem.at[NOFF + i]))
        stores[-1].start()
    for i, h in enumerate(BY_REACH):
        fetches[i].wait()
        k = inner_slot[i]
        add_terms(acc, acc, {h: k}, range(4), mute, [(in2, out2, hal2), (in4, out4, hal4)], True)
        stores.append(store_planes(acc, image, k, 0, 4, True, sem.at[i]))
        stores[-1].start()
    for c in copies + stores:
        c.wait()


def image_main(image_in, part, offsets, mute, snap2, snap4):
    shape = snap2[0].shape
    field = jax.ShapeDtypeStruct((8,) + shape[2:], jnp.float32)
    return pl.pallas_call(
        image_main_kernel,
        out_shape=[
            jax.ShapeDtypeStruct(image_in.shape, jnp.float32), field, field,
            jax.ShapeDtypeStruct((NOFF, 128), jnp.int32),
        ],
        in_specs=[HBM, VMEM, SMEM] + [VMEM] * 7,
        out_specs=[HBM] * 3 + [VMEM],
        scratch_shapes=[
            pltpu.VMEM(part.shape, jnp.float32),
            pltpu.VMEM(part.shape, jnp.float32),
            pltpu.SMEM((NOFF,), jnp.int32),
            pltpu.SemaphoreType.DMA((2 * NOFF,)),
            pltpu.SemaphoreType.DMA((16,)),
        ],
        cost_estimate=CHEAP,
        compiler_params=pltpu.CompilerParams(vmem_limit_bytes=8 * MIB),
        name="image_main",
    )(image_in, part, offsets, mute, *snap2, *snap4)


def image_last_kernel(image_old, part, table, mute, half, other, halo, image, done, sem):
    del image_old
    stores = []
    for reach in range(HMAX, 0, -1):
        pair = {h: table[h + HMAX, 0] for h in (-reach, reach)}
        add_terms(part, done, pair, range(reach), mute, [(half, other, halo)], False)
        for k in pair.values():
            stores.append(store_planes(done, image, k, 0, reach, False, sem.at[len(stores)]))
            stores[-1].start()
    for c in stores:
        c.wait()


def image_last(image, part, table, mute, snap4):
    return pl.pallas_call(
        image_last_kernel,
        out_shape=jax.ShapeDtypeStruct(image.shape, jnp.float32),
        in_specs=[HBM] + [VMEM] * 6,
        out_specs=HBM,
        scratch_shapes=[
            pltpu.VMEM(part.shape, jnp.float32),
            pltpu.SemaphoreType.DMA((NOFF,)),
        ],
        input_output_aliases={0: 0},
        cost_estimate=CHEAP,
        compiler_params=pltpu.CompilerParams(vmem_limit_bytes=8 * MIB),
        name="image_last",
    )(image, part, table, mute, *snap4)


def across_chips(value, start=1, stride=2):
    count = lax.axis_size("blk")
    pairs = [(i, i + 1) for i in range(start, count - 1, stride)]
    return lax.ppermute(value, "blk", pairs + [(b, a) for a, b in pairs])


def within_chip(value):
    return lax.ppermute(value, "blk", [(i, i ^ 1) for i in range(lax.axis_size("blk"))])


def per_device(
    source_prev,
    source_cur,
    receiver_prev,
    receiver_cur,
    coef_horiz,
    coef_vert,
    coef_mixed,
    live_depth,
    offsets,
    image_in,
):
    source_prev, source_cur = source_prev[0], source_cur[0]
    receiver_prev, receiver_cur = receiver_prev[0], receiver_cur[0]
    coefs = [coef_horiz[0], coef_vert[0], coef_mixed[0]]
    image_in = image_in[:, 0]
    rows, depth = source_cur.shape[1:]
    wz, wy = bands(depth, rows)
    depth_ids = lax.broadcasted_iota(jnp.int32, source_cur.shape, 2)
    mute = (depth_ids < live_depth[0][:, :, None]).astype(jnp.float32)

    (out,) = gather([source_cur, receiver_cur], [(0, False, (0, 1))])
    far = across_chips(out)
    (inn,) = gather([source_cur, receiver_cur], [(0, True, (0, 1))])
    near = within_chip(inn)
    base, coef_inn, coef_out, prev_inn = first(
        out, inn, wz, wy, [source_prev, receiver_prev] + coefs
    )
    for n in range(STEPS):
        if n > 0:
            base = half_step(base_kernel, "base", out, inn, prev_out, coef_out, wz, wy)
        new_inn = half_step(inner_kernel, "inner", inn, out, near, prev_inn, coef_inn, wz, wy)
        new_out = finish(far, base, coef_out, wz)
        if n == STEPS // 2:
            snap2 = (inn, out, near)
            part = image_mid(image_in, offsets, mute, out, inn, far)
        prev_inn, prev_out, inn, out = inn, out, new_inn, new_out
        near = within_chip(inn)
        far = across_chips(out)
    image, source_last, receiver_last, table = image_main(
        image_in, part, offsets, mute, snap2, (inn, out, near)
    )
    image = image_last(image, part, table, mute, (out, inn, far))
    return (image[:, None], source_last[None], receiver_last[None])


def solution(mesh):
    in_specs = (
        P(("shots", "blk"), None, None, None),
        P(("shots", "blk"), None, None, None),
        P(("shots", "blk"), None, None, None),
        P(("shots", "blk"), None, None, None),
        P("blk", None, None, None),
        P("blk", None, None, None),
        P("blk", None, None, None),
        P("blk", None, None),
        P(),
        P(None, ("shots", "blk"), None, None, None),
    )
    out_specs = (
        P(None, ("shots", "blk"), None, None, None),
        P(("shots", "blk"), None, None, None),
        P(("shots", "blk"), None, None, None),
    )
    return jax.shard_map(
        per_device, mesh=mesh, in_specs=in_specs, out_specs=out_specs, check_vma=False
    )
```

```python
import functools

import jax
import jax.numpy as jnp
import numpy as np
from jax import lax
from jax.experimental import pallas as pl
from jax.experimental.pallas import tpu as pltpu
from jax.sharding import PartitionSpec as P

STEPS = 4
RAD = 4
HMAX = 4
NOFF = 9

second_w = (-205.0 / 72.0, 8.0 / 5.0, -1.0 / 5.0, 8.0 / 315.0, -1.0 / 560.0)
first_w = (4.0 / 5.0, -1.0 / 5.0, 4.0 / 105.0, -1.0 / 280.0)

VMEM = pl.BlockSpec(memory_space=pltpu.VMEM)
SMEM = pl.BlockSpec(memory_space=pltpu.SMEM)
ANY = pl.BlockSpec(memory_space=pl.ANY)
HBM = pl.BlockSpec(memory_space=pltpu.HBM)
MIB = 1 << 20
BIG = pl.CostEstimate(flops=10000000000, transcendentals=0, bytes_accessed=20000000)
CHEAP = pl.CostEstimate(flops=1, transcendentals=0, bytes_accessed=1)


def parity():
    return lax.rem(lax.axis_index("blk"), 2)


def is_flipped(inner):
    odd = parity()
    return 1 - odd if inner else odd


def natural(plane, flipped):
    return plane + flipped * (7 - 2 * plane)


def at(half, other, halo, field, position):
    if position < 0:
        return pick(halo, field, -1 - position)
    if position < 4:
        return pick(half, field, position)
    return pick(other, field, 7 - position)


def pick(fields, field, plane):
    return fields[field].at[plane] if isinstance(fields, tuple) else fields.at[field, plane]


SCALE = 5040
second_int = tuple(round(SCALE * w) for w in second_w)
first_int = tuple(round(840 * w) for w in first_w)
mixed_w = tuple(SCALE / 840 * w for w in first_w)


def bands(depth, rows):
    d = np.arange(depth)[None, :] - np.arange(depth)[:, None]
    r = np.arange(4 * rows)
    dr = np.where(r[None, :] // rows == r[:, None] // rows, r[None, :] - r[:, None], 99)
    dzz, dz = np.zeros(d.shape), np.zeros(d.shape)
    dyy = np.zeros(dr.shape)
    for k in range(1, 5):
        dzz[np.abs(d) == k] = second_int[k]
        dyy[np.abs(dr) == k] = second_int[k]
        dz[d == -k] = first_int[k - 1]
        dz[d == k] = -first_int[k - 1]
    return jnp.asarray(np.stack([dzz, dz]).astype(jnp.bfloat16)), jnp.asarray(dyy.astype(jnp.bfloat16))


def gather_kernel(plan, n_in, *refs):
    ins, outs, sem = refs[:n_in], refs[n_in:-1], refs[-1]
    copies = []
    for out_id, inner, sources in plan:
        flip = is_flipped(inner)
        for i, src in enumerate(sources):
            for m in range(4):
                copies.append(
                    pltpu.make_async_copy(
                        ins[src].at[natural(m, flip)], outs[out_id].at[i, m], sem.at[len(copies)]
                    )
                )
    for c in copies:
        c.start()
    for c in copies:
        c.wait()


def gather(arrays, plan):
    shape = arrays[0].shape[1:]
    arrays = [pltpu.with_memory_space_constraint(a, pltpu.HBM) for a in arrays]
    return pl.pallas_call(
        functools.partial(gather_kernel, plan, len(arrays)),
        out_shape=[jax.ShapeDtypeStruct((len(s), 4) + shape, jnp.float32) for _, _, s in plan],
        in_specs=[HBM] * len(arrays),
        out_specs=[VMEM] * len(plan),
        scratch_shapes=[pltpu.SemaphoreType.DMA((sum(4 * len(s) for _, _, s in plan),))],
        cost_estimate=BIG,
        compiler_params=pltpu.CompilerParams(vmem_limit_bytes=8 * MIB),
        name="gather",
    )(*arrays)


CHUNK = 16
dot = functools.partial(jnp.dot, preferred_element_type=jnp.float32)


def split(value):
    high = value.astype(jnp.bfloat16)
    return high, (value - high.astype(jnp.float32)).astype(jnp.bfloat16)


def advance(inner, half, other, halo, prev, coef, wz, wy, out, v_hi, v_lo, x_hi, x_lo, horiz):
    rows = half.shape[2]
    sign = (1 - 2 * is_flipped(inner)).astype(jnp.float32)
    wx = [sign * w for w in mixed_w]

    for f in range(2):
        for r in range(0, rows, CHUNK):
            span = pl.ds(r, CHUNK)
            low = 0 if halo is None else -4
            line = {q: at(half, other, halo, f, q)[span] for q in range(low, 8)}
            for m in range(4):
                center = line[m]
                hx = (2.0 * SCALE * second_w[0]) * center
                dx = None
                for k in range(1, 5):
                    up = line[m + k]
                    if m - k in line:
                        both, t = up + line[m - k], up - line[m - k]
                    else:
                        both, t = up, up
                    hx = hx + float(second_int[k]) * both
                    t = wx[k - 1] * t
                    dx = t if dx is None else dx + t
                horiz[f, m, span] = hx
                at_row = pl.ds((f * 4 + m) * rows + r, CHUNK)
                v_hi[at_row], v_lo[at_row] = split(center)
                x_hi[at_row], x_lo[at_row] = split(dx)
        part = pl.ds(f * 4 * rows, 4 * rows)
        vh, vl, xh, xl = v_hi[part], v_lo[part], x_hi[part], x_lo[part]
        zz = dot(vh, wz[0]) + dot(vl, wz[0])
        zx = dot(xh, wz[1]) + dot(xl, wz[1])
        yy = dot(wy[...], vh) + dot(wy[...], vl)
        for m in range(4):
            cut = slice(m * rows, (m + 1) * rows)
            center = half[f, m]
            out[f, m] = (
                2.0 * center
                - prev[f, m]
                + (1.0 / SCALE)
                * (
                    coef[0, m] * (horiz[f, m] + yy[cut])
                    + coef[1, m] * (zz[cut] + (SCALE * second_w[0]) * center)
                    + coef[2, m] * zx[cut]
                )
            )


def inner_kernel(inn, out, near, prev_inn, coef_inn, wz, wy, new_inn, *scratch):
    advance(True, inn, out, near, prev_inn, coef_inn, wz, wy, new_inn, *scratch)


def base_kernel(out, inn, prev_out, coef_out, wz, wy, base, *scratch):
    advance(False, out, inn, None, prev_out, coef_out, wz, wy, base, *scratch)


def first_kernel(
    out, inn, wz, wy, source_prev, receiver_prev, coef_a, coef_b, coef_c,
    base, coef_inn, coef_out, prev_inn, prev_out, sem, *scratch
):
    coefs = (coef_a, coef_b, coef_c)
    prevs = (source_prev, receiver_prev)
    copies = []
    for inner, pairs in (
        (False, [(c, coef_out.at[i]) for i, c in enumerate(coefs)]),
        (False, [(c, prev_out.at[i]) for i, c in enumerate(prevs)]),
        (True, [(c, coef_inn.at[i]) for i, c in enumerate(coefs)]),
        (True, [(c, prev_inn.at[i]) for i, c in enumerate(prevs)]),
    ):
        for source, target in pairs:
            for m in range(4):
                copies.append(
                    pltpu.make_async_copy(
                        source.at[natural(m, is_flipped(inner))], target.at[m], sem.at[len(copies)]
                    )
                )
    for c in copies:
        c.start()
    for c in copies[:20]:
        c.wait()
    advance(False, out, inn, None, prev_out, coef_out, wz, wy, base, *scratch)
    for c in copies[20:]:
        c.wait()


def work_space(rows, depth):
    flat = pltpu.VMEM((8 * rows, depth), jnp.bfloat16)
    return [flat] * 4 + [pltpu.VMEM((2, 4, rows, depth), jnp.float32)]


def first(out, inn, wz, wy, arrays):
    rows, depth = out.shape[2:]
    arrays = [pltpu.with_memory_space_constraint(a, pltpu.HBM) for a in arrays]
    pair = jax.ShapeDtypeStruct((2, 4, rows, depth), jnp.float32)
    three = jax.ShapeDtypeStruct((3, 4, rows, depth), jnp.float32)
    half = pltpu.VMEM((2, 4, rows, depth), jnp.float32)
    return pl.pallas_call(
        first_kernel,
        out_shape=[pair, three, three, pair],
        in_specs=[VMEM] * 4 + [HBM] * 5,
        out_specs=[VMEM] * 4,
        scratch_shapes=[half, pltpu.SemaphoreType.DMA((40,))] + work_space(rows, depth),
        cost_estimate=BIG,
        compiler_params=pltpu.CompilerParams(vmem_limit_bytes=12 * MIB),
        name="first",
    )(out, inn, wz, wy, *arrays)


def half_step(kernel, name, *operands):
    shape = operands[0].shape
    return pl.pallas_call(
        kernel,
        out_shape=jax.ShapeDtypeStruct(shape, jnp.float32),
        in_specs=[VMEM] * len(operands),
        out_specs=VMEM,
        scratch_shapes=work_space(*shape[2:]),
        cost_estimate=CHEAP,
        compiler_params=pltpu.CompilerParams(vmem_limit_bytes=12 * MIB),
        name=name,
    )(*operands)


def finish_kernel(halo, base, coef, wz, out, hi, lo, dz):
    rows = halo.shape[2]
    sign = (1 - 2 * is_flipped(False)).astype(jnp.float32)
    wx = [sign * w / SCALE for w in mixed_w]
    for f in range(2):
        for j in range(4):
            at_row = pl.ds((f * 4 + j) * rows, rows)
            hi[at_row], lo[at_row] = split(halo[f, j])
    dz[...] = dot(hi[...], wz[1]) + dot(lo[...], wz[1])

    for r in range(0, rows, CHUNK):
        span = pl.ds(r, CHUNK)
        for f in range(2):
            h = [halo[f, j, span] for j in range(4)]
            z = [dz[pl.ds((f * 4 + j) * rows + r, CHUNK)] for j in range(4)]
            for m in range(4):
                hx = zx = None
                for k in range(m + 1, 5):
                    t = second_w[k] * h[k - m - 1]
                    hx = t if hx is None else hx + t
                    t = wx[k - 1] * z[k - m - 1]
                    zx = t if zx is None else zx + t
                out[f, m, span] = base[f, m, span] + (coef[0, m, span] * hx - coef[2, m, span] * zx)


def finish(halo, base, coef, wz):
    rows, depth = halo.shape[2:]
    return pl.pallas_call(
        finish_kernel,
        out_shape=jax.ShapeDtypeStruct(halo.shape, jnp.float32),
        in_specs=[VMEM] * 4,
        out_specs=VMEM,
        scratch_shapes=[pltpu.VMEM((8 * rows, depth), jnp.bfloat16)] * 2
        + [pltpu.VMEM((8 * rows, depth), jnp.float32)],
        cost_estimate=CHEAP,
        compiler_params=pltpu.CompilerParams(vmem_limit_bytes=8 * MIB),
        name="finish",
    )(halo, base, coef, wz)


def find_slots(offsets, slots):
    for k in range(NOFF):
        slots[offsets[k]] = k


def slot_of(slots, inner, h):
    return slots[(1 - 2 * is_flipped(inner)) * h + HMAX]


BY_REACH = (-4, 4, -3, 3, -2, 2, -1, 1, 0)


def add_terms(old, new, slots, planes, mute, snaps, inner, straight=False):
    flip = is_flipped(inner)
    rows = old.shape[2]
    chunk = CHUNK
    while chunk < rows and 2 * chunk * len(planes) * len(slots) <= 128:
        chunk *= 2

    def body(i, carry):
        span = pl.ds(i * chunk if straight else pl.multiple_of(i * chunk, chunk), chunk)
        for m in planes:
            local = m + flip * (3 - 2 * m)
            mask = mute[natural(m, flip), span]
            for h, slot in slots.items():
                total = None
                for half, other, halo in snaps:
                    t = at(half, other, halo, 0, m - h)[span] * at(half, other, halo, 1, m + h)[span]
                    total = t if total is None else total + t
                new[slot, local, span] = old[slot, local, span] + mask * total
        return carry

    if straight:
        for i in range(rows // chunk):
            body(i, 0)
    else:
        lax.fori_loop(0, rows // chunk, body, 0)


def store_planes(buffer, image, slot, first, count, inner, sem):
    flip = is_flipped(inner)
    start = first + flip * (4 - 2 * first - count)
    return pltpu.make_async_copy(
        buffer.at[slot, pl.ds(start, count)], image.at[slot, pl.ds(4 * flip + start, count)], sem
    )


def image_mid_kernel(image_in, offsets, mute, half, other, halo, acc, slots, sem):
    find_slots(offsets, slots)
    near = pl.ds(4 * is_flipped(False), 4)
    slot = [slot_of(slots, False, h) for h in BY_REACH]
    copies = [
        pltpu.make_async_copy(image_in.at[k, near], acc.at[k], sem.at[i])
        for i, k in enumerate(slot)
    ]
    for c in copies:
        c.start()
    for i, h in enumerate(BY_REACH):
        copies[i].wait()
        add_terms(acc, acc, {h: slot[i]}, range(4), mute, [(half, other, halo)], False)


def image_mid(image_in, offsets, mute, half, other, halo):
    shape = (NOFF, 4) + half.shape[2:]
    return pl.pallas_call(
        image_mid_kernel,
        out_shape=jax.ShapeDtypeStruct(shape, jnp.float32),
        in_specs=[HBM, SMEM] + [VMEM] * 4,
        out_specs=VMEM,
        scratch_shapes=[pltpu.SMEM((NOFF,), jnp.int32), pltpu.SemaphoreType.DMA((NOFF,))],
        cost_estimate=CHEAP,
        compiler_params=pltpu.CompilerParams(vmem_limit_bytes=8 * MIB),
        name="image_mid",
    )(image_in, offsets, mute, half, other, halo)


def image_main_kernel(
    image_in, part, offsets, mute, in2, out2, hal2, in4, out4, hal4,
    image, src, rec, table, acc, done, slots, sem, sems,
):
    find_slots(offsets, slots)
    inner_half = pl.ds(4 * is_flipped(True), 4)
    inner_slot = [slot_of(slots, True, h) for h in BY_REACH]
    outer_slot = [slot_of(slots, False, h) for h in BY_REACH]
    for h, k in zip(BY_REACH, outer_slot):
        table[pl.ds(h + HMAX, 1)] = jnp.full((1, table.shape[1]), k, jnp.int32)
    fetches = [
        pltpu.make_async_copy(image_in.at[k, inner_half], acc.at[k], sem.at[i])
        for i, k in enumerate(inner_slot)
    ]
    for c in fetches:
        c.start()
    copies = []
    for inner, field4 in ((True, in4), (False, out4)):
        for f, last in ((0, src), (1, rec)):
            for m in range(4):
                copies.append(
                    pltpu.make_async_copy(
                        field4.at[f, m], last.at[natural(m, is_flipped(inner))], sems.at[len(copies)]
                    )
                )
    for c in copies:
        c.start()
    stores = []
    for i, h in enumerate(BY_REACH):
        reach = abs(h)
        if reach == 4:
            continue
        k = outer_slot[i]
        add_terms(part, done, {h: k}, range(reach, 4), mute, [(out4, in4, None)], False)
        stores.append(store_planes(done, image, k, reach, 4 - reach, False, sem.at[NOFF + i]))
        stores[-1].start()
    for i, h in enumerate(BY_REACH):
        fetches[i].wait()
        k = inner_slot[i]
        add_terms(acc, acc, {h: k}, range(4), mute, [(in2, out2, hal2), (in4, out4, hal4)], True)
        stores.append(store_planes(acc, image, k, 0, 4, True, sem.at[i]))
        stores[-1].start()
    for c in copies + stores:
        c.wait()


def image_main(image_in, part, offsets, mute, snap2, snap4):
    shape = snap2[0].shape
    field = jax.ShapeDtypeStruct((8,) + shape[2:], jnp.float32)
    return pl.pallas_call(
        image_main_kernel,
        out_shape=[
            jax.ShapeDtypeStruct(image_in.shape, jnp.float32), field, field,
            jax.ShapeDtypeStruct((NOFF, 128), jnp.int32),
        ],
        in_specs=[HBM, VMEM, SMEM] + [VMEM] * 7,
        out_specs=[HBM] * 3 + [VMEM],
        scratch_shapes=[
            pltpu.VMEM(part.shape, jnp.float32),
            pltpu.VMEM(part.shape, jnp.float32),
            pltpu.SMEM((NOFF,), jnp.int32),
            pltpu.SemaphoreType.DMA((2 * NOFF,)),
            pltpu.SemaphoreType.DMA((16,)),
        ],
        cost_estimate=CHEAP,
        compiler_params=pltpu.CompilerParams(vmem_limit_bytes=8 * MIB),
        name="image_main",
    )(image_in, part, offsets, mute, *snap2, *snap4)


def image_last_kernel(image_old, part, table, mute, half, other, halo, image, done, sem):
    del image_old
    stores = []
    slot = {h: table[h + HMAX, 0] for h in range(-HMAX, HMAX + 1)}
    for reach in range(HMAX, 0, -1):
        pair = {h: slot[h] for h in (-reach, reach)}
        add_terms(part, done, pair, range(reach), mute, [(half, other, halo)], False, True)
        for k in pair.values():
            stores.append(store_planes(done, image, k, 0, reach, False, sem.at[len(stores)]))
            stores[-1].start()
    for c in stores:
        c.wait()


def image_last(image, part, table, mute, snap4):
    return pl.pallas_call(
        image_last_kernel,
        out_shape=jax.ShapeDtypeStruct(image.shape, jnp.float32),
        in_specs=[HBM] + [VMEM] * 6,
        out_specs=HBM,
        scratch_shapes=[
            pltpu.VMEM(part.shape, jnp.float32),
            pltpu.SemaphoreType.DMA((NOFF,)),
        ],
        input_output_aliases={0: 0},
        cost_estimate=CHEAP,
        compiler_params=pltpu.CompilerParams(vmem_limit_bytes=8 * MIB),
        name="image_last",
    )(image, part, table, mute, *snap4)


def across_chips(value, start=1, stride=2):
    count = lax.axis_size("blk")
    pairs = [(i, i + 1) for i in range(start, count - 1, stride)]
    return lax.ppermute(value, "blk", pairs + [(b, a) for a, b in pairs])


def within_chip(value):
    return lax.ppermute(value, "blk", [(i, i ^ 1) for i in range(lax.axis_size("blk"))])


def per_device(
    source_prev,
    source_cur,
    receiver_prev,
    receiver_cur,
    coef_horiz,
    coef_vert,
    coef_mixed,
    live_depth,
    offsets,
    image_in,
):
    source_prev, source_cur = source_prev[0], source_cur[0]
    receiver_prev, receiver_cur = receiver_prev[0], receiver_cur[0]
    coefs = [coef_horiz[0], coef_vert[0], coef_mixed[0]]
    image_in = image_in[:, 0]
    rows, depth = source_cur.shape[1:]
    wz, wy = bands(depth, rows)
    depth_ids = lax.broadcasted_iota(jnp.int32, source_cur.shape, 2)
    mute = (depth_ids < live_depth[0][:, :, None]).astype(jnp.float32)

    (out,) = gather([source_cur, receiver_cur], [(0, False, (0, 1))])
    far = across_chips(out)
    (inn,) = gather([source_cur, receiver_cur], [(0, True, (0, 1))])
    near = within_chip(inn)
    base, coef_inn, coef_out, prev_inn = first(
        out, inn, wz, wy, [source_prev, receiver_prev] + coefs
    )
    for n in range(STEPS):
        if n > 0:
            base = half_step(base_kernel, "base", out, inn, prev_out, coef_out, wz, wy)
        new_inn = half_step(inner_kernel, "inner", inn, out, near, prev_inn, coef_inn, wz, wy)
        new_out = finish(far, base, coef_out, wz)
        if n == STEPS // 2:
            snap2 = (inn, out, near)
            part = image_mid(image_in, offsets, mute, out, inn, far)
        prev_inn, prev_out, inn, out = inn, out, new_inn, new_out
        near = within_chip(inn)
        far = across_chips(out)
    image, source_last, receiver_last, table = image_main(
        image_in, part, offsets, mute, snap2, (inn, out, near)
    )
    image = image_last(image, part, table, mute, (out, inn, far))
    return (image[:, None], source_last[None], receiver_last[None])


def solution(mesh):
    in_specs = (
        P(("shots", "blk"), None, None, None),
        P(("shots", "blk"), None, None, None),
        P(("shots", "blk"), None, None, None),
        P(("shots", "blk"), None, None, None),
        P("blk", None, None, None),
        P("blk", None, None, None),
        P("blk", None, None, None),
        P("blk", None, None),
        P(),
        P(None, ("shots", "blk"), None, None, None),
    )
    out_specs = (
        P(None, ("shots", "blk"), None, None, None),
        P(("shots", "blk"), None, None, None),
        P(("shots", "blk"), None, None, None),
    )
    return jax.shard_map(
        per_device, mesh=mesh, in_specs=in_specs, out_specs=out_specs, check_vma=False
    )
```
